32 devices in a mesh: groups: 2 (over y), gx: 8 (over z, x), gy: 2 (over core).
Axes of the slice: x: 2, y: 2, z: 4, core: 2. Of those that a mesh axis runs over, the one named last changes fastest.
Arguments:
- voxels: bfloat16 [16, 128, 128, 64], P(('groups', 'gx'), 'gy'), parts along dimension 0, may hold values from -6 to 6
- occupancy: int32 [16, 128, 128], P(('groups', 'gx'), 'gy'), parts along dimension 0, may hold values 0 or 1
- row_weights: bfloat16 [8, 64], P('gx'), may hold values from -2 to 2
- column_weights: bfloat16 [128, 64], P('gy'), may hold values from -0.5 to 0.5
- depth_weights: bfloat16 [128, 64], replicated, may hold values from -0.5 to 0.5
- plane_kernels: bfloat16 [3, 2, 3, 3, 64, 64], replicated, may hold values from -0.25 to 0.25
- expand_weight: bfloat16 [64, 128], replicated, may hold values from -0.75 to 0.75
- shrink_weight: bfloat16 [128, 64], replicated, may hold values from -1 to 1
Outputs:
- updated: bfloat16 [16, 128, 128, 64], P(('groups', 'gx'), 'gy'), parts along dimension 0
The draws below stay inside these ranges and needn't reach their ends.
There are 2 independent parts, one for each index of `groups`. The reference program is written for one: setup_inputs(seed, part) draws one part's arguments, and reference() takes and returns one part's arrays. A program takes and returns all parts, laid end to end along the dimension named above; an argument that names none is the same for every part. Nothing has to cross between parts.
All inputs are finite; a program needn't handle non-finite values. No bound on the sum of `occupancy` on one device may be relied on, other than what follows from the above.
Results may differ from the reference program's by a relative error of at most 0.015.
Values may be sent and summed in bfloat16 or wider, within the bound.
A program may use at most 64 MiB of HBM per device.

```python
import jax
import jax.numpy as jnp
from jax import lax

C = 64
H = 128
Z = 128
X = 8
Y = 128


def set_ends(result, own_key, smallest, largest):
    longest = result.shape.index(max(result.shape))
    spots = []
    for shift in (0, 1):
        where = [jax.random.randint(jax.random.fold_in(own_key, axis), (), 0, length) for axis, length in enumerate(result.shape)]
        where[longest] = (where[longest] + shift) % result.shape[longest]
        spots.append(tuple(where))
    return result.at[spots[0]].set(smallest).at[spots[1]].set(largest)


def levels(stream_key, extent, shards, low, high):
    level = 1.0
    for position, blocks in shards:
        draws = jax.random.uniform(jax.random.fold_in(jax.random.fold_in(stream_key, 6), position), (blocks,), jnp.float32, low / len(shards), high / len(shards))
        level = level * jnp.repeat(jnp.exp(draws), extent[position] // blocks).reshape((-1,) + (1,) * (len(extent) - 1 - position))
    return level


def centred(key, shape, spread, limit, cuts=(), dtype=jnp.bfloat16):
    entries = jax.random.normal(key, shape, jnp.float32) * spread
    if len(cuts) > 0:
        entries = levels(key, shape, cuts, -0.22, 0.18) * entries
    return jnp.clip(entries, min=-limit, max=limit).astype(dtype)


def setup_inputs(seed: int = 0, part: int = 0) -> dict:
    streams_of = jax.random.split(jax.random.key(seed), 9)
    part_keys = jax.random.split(jax.random.fold_in(streams_of[8], part), 9)
    voxels = centred(part_keys[0], (X, Y, Z, C), 1.0, 6.0, ((0, 8), (1, 2)))
    occupancy = set_ends((jax.random.randint(part_keys[1], (X, Y, Z), 0, 2) < 1).astype(jnp.int32), jax.random.fold_in(part_keys[1], 1), 0, 1)
    row_weights = centred(streams_of[2], (X, C), X ** -0.5, 2.0, ((0, 8),))
    column_weights = centred(streams_of[3], (Y, C), Y ** -0.5, 0.5, ((0, 2),))
    depth_weights = centred(streams_of[4], (Z, C), Z ** -0.5, 0.5)
    plane_kernels = centred(streams_of[5], (3, 2, 3, 3, C, C), (9 * C) ** -0.5, 0.25)
    expand_weight = centred(streams_of[6], (C, H), C ** -0.5, 0.75)
    shrink_weight = centred(streams_of[7], (H, C), (H // 4) ** -0.5, 1.0)
    return {"voxels": voxels, "occupancy": occupancy, "row_weights": row_weights, "column_weights": column_weights, "depth_weights": depth_weights, "plane_kernels": plane_kernels, "expand_weight": expand_weight, "shrink_weight": shrink_weight}


product_scale = 8.0


def conv_same(plane, kernel):
    rows = plane.shape[0]
    cols = plane.shape[1]
    padded = jnp.pad(plane.astype(jnp.float32), ((1, 1), (1, 1), (0, 0)))
    total = jnp.zeros((rows, cols, kernel.shape[-1]), jnp.float32)
    for row_off in range(3):
        for col_off in range(3):
            window = padded[row_off:row_off + rows, col_off:col_off + cols]
            total = total + jnp.einsum("ijc,co->ijo", window, kernel[row_off, col_off].astype(jnp.float32))
    return total


def plane_block(plane, kernels):
    inner = jax.nn.silu(conv_same(plane, kernels[0])).astype(jnp.bfloat16)
    return conv_same(inner, kernels[1]).astype(jnp.bfloat16)


def reference(voxels, occupancy, row_weights, column_weights, depth_weights, plane_kernels, expand_weight, shrink_weight):
    features = voxels * occupancy.astype(jnp.bfloat16)[..., None]
    widened = features.astype(jnp.float32)
    xy_plane = jnp.einsum("xyzc,zc->xyc", widened, depth_weights.astype(jnp.float32)).astype(jnp.bfloat16)
    xz_plane = jnp.einsum("xyzc,yc->xzc", widened, column_weights.astype(jnp.float32)).astype(jnp.bfloat16)
    yz_plane = jnp.einsum("xyzc,xc->yzc", widened, row_weights.astype(jnp.float32)).astype(jnp.bfloat16)
    xy_out = plane_block(xy_plane, plane_kernels[0])
    xz_out = plane_block(xz_plane, plane_kernels[1])
    yz_out = plane_block(yz_plane, plane_kernels[2])
    expand_wide = expand_weight.astype(jnp.float32)
    shrink_wide = shrink_weight.astype(jnp.float32)

    def per_slice(items):
        feature_slice, xy_row, xz_row = items
        product = xy_row.astype(jnp.float32)[:, None, :] * xz_row.astype(jnp.float32)[None, :, :]
        product = product * yz_out.astype(jnp.float32)
        mixed = (product_scale * product).astype(jnp.bfloat16).astype(jnp.float32)
        hidden = jax.nn.silu(jnp.einsum("yzc,ch->yzh", mixed, expand_wide)).astype(jnp.bfloat16)
        branch = jnp.einsum("yzh,hc->yzc", hidden.astype(jnp.float32), shrink_wide)
        return (feature_slice.astype(jnp.float32) + branch).astype(jnp.bfloat16)

    return lax.map(per_slice, (features, xy_out, xz_out))
```

```python
import functools

import jax
import jax.numpy as jnp
from jax import lax
from jax.experimental import pallas as pl
from jax.experimental.pallas import tpu as pltpu
from jax.sharding import PartitionSpec as P

MESH = pl.DeviceIdType.MESH
reach = 2

product_scale = 8.0


def with_halo(cells, sides, width):
    for axis, dim in sides:
        count = lax.axis_size(axis)
        ends = count - 1
        head = lax.slice_in_dim(cells, 0, width, axis=dim)
        tail = lax.slice_in_dim(cells, cells.shape[dim] - width, cells.shape[dim], axis=dim)
        cells = jnp.concatenate(
            [
                lax.ppermute(tail, axis, [(i, (i + 1) % count) for i in range(ends)]),
                cells,
                lax.ppermute(head, axis, [((i + 1) % count, i) for i in range(ends)]),
            ],
            axis=dim,
        )
    return cells


def conv_valid(padded, kernel):
    rows = padded.shape[0] - 2
    cols = padded.shape[1] - 2
    total = jnp.zeros((rows, cols, kernel.shape[-1]), jnp.float32)
    for row_off in range(3):
        for col_off in range(3):
            window = padded[row_off : row_off + rows, col_off : col_off + cols]
            total = total + jnp.einsum(
                "ijc,co->ijo", window, kernel[row_off, col_off], preferred_element_type=jnp.float32
            )
    return total


def plane_block(plane, kernels, extend):
    inner = jax.nn.silu(conv_valid(extend(plane), kernels[0])).astype(jnp.bfloat16)
    return conv_valid(extend(inner), kernels[1]).astype(jnp.bfloat16)


def rim_xy(plane):
    return with_halo(plane, (("gx", 0), ("gy", 1)), 1)


def rim_xz(plane):
    padded = with_halo(plane, (("gx", 0),), 1)
    return jnp.pad(padded, ((0, 0), (1, 1), (0, 0)))


def rim_yz(plane):
    padded = with_halo(plane, (("gy", 0),), 1)
    return jnp.pad(padded, ((0, 0), (1, 1), (0, 0)))


def conv_row(window, weight):
    taps = jnp.dot(weight, window, preferred_element_type=jnp.float32)
    chans = taps.shape[0] // 3
    cols = taps.shape[1]
    lane = lax.broadcasted_iota(jnp.int32, (chans, cols), 1)
    left = pltpu.roll(taps[:chans], 1, 1)
    right = pltpu.roll(taps[2 * chans :], cols - 1, 1)
    left = jnp.where(lane == 0, 0.0, left)
    right = jnp.where(lane == cols - 1, 0.0, right)
    return taps[chans : 2 * chans] + left + right


def silu(v):
    return v / (1.0 + jnp.exp(-v))


def planes_kernel(
    n, part, rows_in, weights, yz_out, xy_out, xz_out,
    pair_in, pair_sum, line_in, yz_plane, yz_inner, row_slots, row_plane, row_inner,
    pair_s, pair_r, line_s, line_r, halo_s, halo_r, row_s, row_r, spread_s, spread_r, cross_s, cross_r,
):
    me = lax.axis_index("gx")
    g = lax.axis_index("gy")
    m = n // 2
    a = me // 2
    b = me % 2
    count, chans, cols = part.shape
    rows = count // n

    def piece(bb, aa):
        return bb * m + aa + bb * (m - 1 - 2 * aa)

    def owner(j):
        bb = j // m
        aa = j % m
        return (aa + bb * (m - 1 - 2 * aa)) * 2 + bb

    def span(j):
        return pl.ds(j * rows, rows)

    barrier = pltpu.get_barrier_semaphore()
    for step in range(1, 2 * n):
        spot = (me * 2 + g + step) % (2 * n)
        pl.semaphore_signal(barrier, inc=1, device_id={"gx": spot // 2, "gy": spot % 2}, device_id_type=MESH)
    pl.semaphore_wait(barrier, 2 * n - 1)

    row_copies = []
    for dx in range(-reach, reach + 1):
        for dg in range(2):
            if dx == 0 and dg == 0:
                continue
            slot = reach - dx
            copy = pltpu.make_async_remote_copy(
                src_ref=rows_in,
                dst_ref=row_slots.at[slot, dg],
                send_sem=row_s.at[slot, dg],
                recv_sem=row_r.at[slot, dg],
                device_id={"gx": jnp.clip(me + dx, 0, n - 1), "gy": (g + dg) % 2},
                device_id_type=MESH,
            )
            row_copies.append((dx, copy))

    order = list(range(1, m)) + [0]
    pair_copies = []
    for t, off in enumerate(order):
        aa = (a + off) % m
        pair_copies.append(
            pltpu.make_async_remote_copy(
                src_ref=part.at[span(piece(1 - b, aa))],
                dst_ref=pair_in.at[t],
                send_sem=pair_s.at[t],
                recv_sem=pair_r.at[t],
                device_id={"gx": a * 2 + 1 - b},
                device_id_type=MESH,
            )
        )
    pair_copies[0].start()
    for dx, copy in row_copies:
        pl.when((me + dx >= 0) & (me + dx < n))(copy.start)
    for copy in pair_copies[1:]:
        copy.start()

    line_copies = []
    for t, off in enumerate(order[:-1]):
        aa = (a + off) % m
        pair_copies[t].wait_recv()
        mine = part[span(piece(b, aa))].astype(jnp.float32)
        pair_sum[t] = (mine + pair_in[t].astype(jnp.float32)).astype(jnp.bfloat16)
        copy = pltpu.make_async_remote_copy(
            src_ref=pair_sum.at[t],
            dst_ref=line_in.at[t],
            send_sem=line_s.at[t],
            recv_sem=line_r.at[t],
            device_id={"gx": aa * 2 + b},
            device_id_type=MESH,
        )
        copy.start()
        line_copies.append(copy)

    for dx, copy in row_copies:
        pl.when((me - dx >= 0) & (me - dx < n))(copy.wait_recv)
    planes = rows_in.shape[0]
    for s in range(2 * reach + 1):
        at = me + s - reach
        inside = (at >= 0) & (at < n)
        here = pl.ds(s * chans, chans)

        @pl.when(inside)
        def _():
            first = rows_in[...] if s == reach else row_slots[s, 0]
            total = first.astype(jnp.float32) + row_slots[s, 1].astype(jnp.float32)
            row_plane[:, here, :] = total.astype(jnp.bfloat16)

        @pl.when(jnp.logical_not(inside))
        def _():
            row_plane[:, here, :] = jnp.zeros((planes, chans, cols), jnp.bfloat16)

    for p in range(planes):
        for s in range(3):
            at = me + s - 1
            keep = ((at >= 0) & (at < n)).astype(jnp.float32)
            inner = silu(conv_row(row_plane[p, s * chans : (s + 3) * chans, :], weights[p, 0]))
            row_inner[p, s * chans : (s + 1) * chans, :] = (inner * keep).astype(jnp.bfloat16)
    xy_row = conv_row(row_inner[0], weights[0, 1]).astype(jnp.bfloat16)
    half = xy_out.shape[1]
    xy_out[...] = jnp.where(g == 0, xy_row[:, :half], xy_row[:, half:])
    xz_out[...] = conv_row(row_inner[1], weights[1, 1]).astype(jnp.bfloat16)

    mine_at = piece(b, a)
    pair_copies[m - 1].wait_recv()
    for copy in line_copies:
        copy.wait_recv()
    total = part[span(mine_at)].astype(jnp.float32) + pair_in[m - 1].astype(jnp.float32)
    for t in range(m - 1):
        total = total + line_in[t].astype(jnp.float32)
    yz_plane[pl.ds(reach * chans, rows * chans), :] = total.astype(jnp.bfloat16).reshape(rows * chans, cols)

    place = g * n + mine_at
    last = 2 * n - 1
    edge = reach * chans
    before = jnp.maximum(place - 1, 0)
    after = jnp.minimum(place + 1, last)
    up = pltpu.make_async_remote_copy(
        src_ref=yz_plane.at[pl.ds(edge, edge)],
        dst_ref=yz_plane.at[pl.ds(edge + rows * chans, edge)],
        send_sem=halo_s.at[0],
        recv_sem=halo_r.at[0],
        device_id={"gx": owner(before % n), "gy": before // n},
        device_id_type=MESH,
    )
    down = pltpu.make_async_remote_copy(
        src_ref=yz_plane.at[pl.ds(rows * chans, edge)],
        dst_ref=yz_plane.at[pl.ds(0, edge)],
        send_sem=halo_s.at[1],
        recv_sem=halo_r.at[1],
        device_id={"gx": owner(after % n), "gy": after // n},
        device_id_type=MESH,
    )
    pl.when(place > 0)(up.start)
    pl.when(place < last)(down.start)

    @pl.when(place == 0)
    def _():
        yz_plane[pl.ds(0, edge), :] = jnp.zeros((edge, cols), jnp.bfloat16)

    @pl.when(place == last)
    def _():
        yz_plane[pl.ds(edge + rows * chans, edge), :] = jnp.zeros((edge, cols), jnp.bfloat16)

    def inner_row(i, keep):
        window = yz_plane[pl.ds(pl.multiple_of(i * chans, chans), 3 * chans), :]
        inner = silu(conv_row(window, weights[2, 0])) * keep
        yz_inner[pl.ds(pl.multiple_of(i * chans, chans), chans), :] = inner.astype(jnp.bfloat16)

    for i in range(reach, rows):
        inner_row(i, 1.0)
    pl.when(place < last)(up.wait_recv)
    pl.when(place > 0)(down.wait_recv)
    for i in list(range(reach)) + list(range(rows, rows + 2)):
        keep = 1.0
        if i == 0:
            keep = (place > 0).astype(jnp.float32)
        if i == rows + 1:
            keep = (place < last).astype(jnp.float32)
        inner_row(i, keep)
    for r in range(rows):
        done = conv_row(yz_inner[pl.ds(r * chans, 3 * chans), :], weights[2, 1])
        yz_out[mine_at * rows + r] = done.astype(jnp.bfloat16)

    def give(j, send, recv, target):
        return pltpu.make_async_remote_copy(
            src_ref=yz_out.at[span(j)],
            dst_ref=yz_out.at[span(j)],
            send_sem=send,
            recv_sem=recv,
            device_id={"gx": target},
            device_id_type=MESH,
        )

    partner = a * 2 + 1 - b
    sends = []
    for t in range(1, m):
        copy = give(mine_at, spread_s.at[t], spread_r.at[t], ((a + t) % m) * 2 + b)
        copy.start()
        sends.append(copy)
    copy = give(mine_at, cross_s.at[0], cross_r.at[0], partner)
    copy.start()
    sends.append(copy)
    for t in range(1, m):
        j = piece(b, (a + m - t) % m)
        give(j, spread_s.at[t], spread_r.at[t], partner).wait_recv()
        copy = give(j, cross_s.at[t], cross_r.at[t], partner)
        copy.start()
        sends.append(copy)
    for t in range(m):
        give(piece(1 - b, (a + m - t) % m), cross_s.at[t], cross_r.at[t], partner).wait_recv()
    for copy in sends + pair_copies + line_copies:
        copy.wait_send()
    for dx, copy in row_copies:
        pl.when((me + dx >= 0) & (me + dx < n))(copy.wait_send)
    pl.when(place > 0)(up.wait_send)
    pl.when(place < last)(down.wait_send)


def run_planes(part, rows_in, weights):
    n = lax.axis_size("gx")
    m = n // 2
    count, chans, cols = part.shape
    rows = count // n
    planes = rows_in.shape[0]
    wide = 2 * reach + 1
    bf = jnp.bfloat16
    dma = pltpu.SemaphoreType.DMA
    return pl.pallas_call(
        functools.partial(planes_kernel, n),
        out_shape=(
            jax.ShapeDtypeStruct(part.shape, bf),
            jax.ShapeDtypeStruct((chans, count), bf),
            jax.ShapeDtypeStruct((chans, cols), bf),
        ),
        in_specs=[pl.BlockSpec(memory_space=pltpu.VMEM)] * 3,
        out_specs=(pl.BlockSpec(memory_space=pltpu.VMEM),) * 3,
        scratch_shapes=[
            pltpu.VMEM((m, rows, chans, cols), bf),
            pltpu.VMEM((m, rows, chans, cols), bf),
            pltpu.VMEM((m, rows, chans, cols), bf),
            pltpu.VMEM(((rows + 4) * chans, cols), bf),
            pltpu.VMEM(((rows + 2) * chans, cols), bf),
            pltpu.VMEM((wide, 2, planes, chans, cols), bf),
            pltpu.VMEM((planes, wide * chans, cols), bf),
            pltpu.VMEM((planes, 3 * chans, cols), bf),
            dma((m,)), dma((m,)), dma((m,)), dma((m,)), dma((2,)), dma((2,)),
            dma((wide, 2)), dma((wide, 2)), dma((m,)), dma((m,)), dma((m,)), dma((m,)),
        ],
        compiler_params=pltpu.CompilerParams(collective_id=0, has_side_effects=True),
    )(part, rows_in, weights)


def fits(voxels):
    n = lax.axis_size("gx")
    sides = lax.axis_size("gy")
    xs, ys, zs, _ = voxels.shape
    return xs == 1 and sides == 2 and n % 2 == 0 and n >= 4 and ys % n == 0 and ys // n >= reach and 2 * ys == zs


def fused_planes(features, row_weights, column_weights, depth_weights, plane_kernels):
    ys = features.shape[1]
    xy_plane = jnp.einsum(
        "xyzc,zc->xyc", features, depth_weights, preferred_element_type=jnp.float32
    )[0].T
    xz_part = jnp.einsum(
        "xyzc,yc->xzc", features, column_weights, preferred_element_type=jnp.float32
    )[0].T
    part = (features[0].astype(jnp.float32) * row_weights[0].astype(jnp.float32)).astype(jnp.bfloat16)
    part = part.transpose(0, 2, 1)
    g = lax.axis_index("gy")
    blank = jnp.zeros_like(xy_plane)
    xy_wide = jnp.concatenate(
        [jnp.where(g == 0, xy_plane, blank), jnp.where(g == 0, blank, xy_plane)], axis=1
    )
    rows_in = jnp.stack([xy_wide, xz_part]).astype(jnp.bfloat16)
    planes, layers, _, _, chans, outs = plane_kernels.shape
    weights = plane_kernels.transpose(0, 1, 3, 5, 2, 4).reshape(planes, layers, 3 * outs, 3 * chans)
    yz_out, xy_out, xz_out = run_planes(part, rows_in, weights)
    return xy_out.T[None], xz_out.T[None], yz_out.transpose(0, 2, 1)


def plain_planes(features, row_weights, column_weights, depth_weights, plane_kernels):
    xy_plane = jnp.einsum(
        "xyzc,zc->xyc", features, depth_weights, preferred_element_type=jnp.float32
    ).astype(jnp.bfloat16)
    xz_part = jnp.einsum(
        "xyzc,yc->xzc", features, column_weights, preferred_element_type=jnp.float32
    )
    yz_part = jnp.einsum("xyzc,xc->yzc", features, row_weights, preferred_element_type=jnp.float32)
    xy_out = plane_block(xy_plane, plane_kernels[0], rim_xy)
    xz_plane = lax.psum(xz_part, "gy").astype(jnp.bfloat16)
    xz_out = plane_block(xz_plane, plane_kernels[1], rim_xz)
    yz_plane = lax.psum(yz_part, "gx").astype(jnp.bfloat16)
    yz_out = plane_block(yz_plane, plane_kernels[2], rim_yz)
    return xy_out, xz_out, yz_out


def shards(
    voxels,
    occupancy,
    row_weights,
    column_weights,
    depth_weights,
    plane_kernels,
    expand_weight,
    shrink_weight,
):
    features = voxels * occupancy.astype(jnp.bfloat16)[..., None]
    make = fused_planes if fits(voxels) else plain_planes
    xy_out, xz_out, yz_out = make(features, row_weights, column_weights, depth_weights, plane_kernels)
    product = xy_out.astype(jnp.float32)[:, :, None, :] * xz_out.astype(jnp.float32)[:, None, :, :]
    product = product * yz_out.astype(jnp.float32)[None, :, :, :]
    mixed = (product_scale * product).astype(jnp.bfloat16)
    hidden = jax.nn.silu(
        jnp.einsum("xyzc,ch->xyzh", mixed, expand_weight, preferred_element_type=jnp.float32)
    ).astype(jnp.bfloat16)
    branch = jnp.einsum("xyzh,hc->xyzc", hidden, shrink_weight, preferred_element_type=jnp.float32)
    return (features.astype(jnp.float32) + branch).astype(jnp.bfloat16)


def solution(mesh):
    in_specs = (
        P(("groups", "gx"), "gy", None, None),
        P(("groups", "gx"), "gy", None),
        P("gx", None),
        P("gy", None),
        P(),
        P(),
        P(),
        P(),
    )
    out_specs = P(("groups", "gx"), "gy", None, None)
    return jax.shard_map(shards, mesh=mesh, in_specs=in_specs, out_specs=out_specs, check_vma=False)
```

```python
import functools

import jax
import jax.numpy as jnp
from jax import lax
from jax.experimental import pallas as pl
from jax.experimental.pallas import tpu as pltpu
from jax.sharding import PartitionSpec as P

MESH = pl.DeviceIdType.MESH
reach = 2

product_scale = 8.0


def with_halo(cells, sides, width):
    for axis, dim in sides:
        count = lax.axis_size(axis)
        ends = count - 1
        head = lax.slice_in_dim(cells, 0, width, axis=dim)
        tail = lax.slice_in_dim(cells, cells.shape[dim] - width, cells.shape[dim], axis=dim)
        cells = jnp.concatenate(
            [
                lax.ppermute(tail, axis, [(i, (i + 1) % count) for i in range(ends)]),
                cells,
                lax.ppermute(head, axis, [((i + 1) % count, i) for i in range(ends)]),
            ],
            axis=dim,
        )
    return cells


def conv_valid(padded, kernel):
    rows = padded.shape[0] - 2
    cols = padded.shape[1] - 2
    total = jnp.zeros((rows, cols, kernel.shape[-1]), jnp.float32)
    for row_off in range(3):
        for col_off in range(3):
            window = padded[row_off : row_off + rows, col_off : col_off + cols]
            total = total + jnp.einsum(
                "ijc,co->ijo", window, kernel[row_off, col_off], preferred_element_type=jnp.float32
            )
    return total


def plane_block(plane, kernels, extend):
    inner = jax.nn.silu(conv_valid(extend(plane), kernels[0])).astype(jnp.bfloat16)
    return conv_valid(extend(inner), kernels[1]).astype(jnp.bfloat16)


def rim_xy(plane):
    return with_halo(plane, (("gx", 0), ("gy", 1)), 1)


def rim_xz(plane):
    padded = with_halo(plane, (("gx", 0),), 1)
    return jnp.pad(padded, ((0, 0), (1, 1), (0, 0)))


def rim_yz(plane):
    padded = with_halo(plane, (("gy", 0),), 1)
    return jnp.pad(padded, ((0, 0), (1, 1), (0, 0)))


def conv_row(window, weight):
    taps = jnp.dot(weight, window, preferred_element_type=jnp.float32)
    chans = taps.shape[0] // 3
    cols = taps.shape[1]
    lane = lax.broadcasted_iota(jnp.int32, (chans, cols), 1)
    left = pltpu.roll(taps[:chans], 1, 1)
    right = pltpu.roll(taps[2 * chans :], cols - 1, 1)
    left = jnp.where(lane == 0, 0.0, left)
    right = jnp.where(lane == cols - 1, 0.0, right)
    return taps[chans : 2 * chans] + left + right


def silu(v):
    return v / (1.0 + jnp.exp(-v))


def identity(size):
    row = lax.broadcasted_iota(jnp.int32, (size, size), 0)
    col = lax.broadcasted_iota(jnp.int32, (size, size), 1)
    return jnp.where(row == col, 1.0, 0.0)


def flipped(x):
    eye = identity(x.shape[1]).astype(x.dtype)
    return lax.dot_general(eye, x, (((1,), (1,)), ((), ())), preferred_element_type=jnp.float32)


def column(x, at):
    lane = lax.broadcasted_iota(jnp.int32, x.shape, 1)
    return jnp.sum(jnp.where(lane == at, x, 0.0), axis=1, keepdims=True)


def block_kernel(
    n, voxels, occupancy, row_weights, column_weights, depth_weights, plane_kernels, expand, shrink, updated,
    part, rows_in, weights, wide, yz_out, xy_out, xz_out, row_sums, turned,
    pair_in, pair_sum, line_in, yz_plane, yz_inner, row_slots, row_plane, row_inner,
    pair_s, pair_r, line_s, line_r, halo_s, halo_r, row_s, row_r, spread_s, spread_r, cross_s, cross_r,
):
    me = lax.axis_index("gx")
    g = lax.axis_index("gy")
    m = n // 2
    a = me // 2
    b = me % 2
    count, chans, cols = part.shape
    rows = count // n
    bf = jnp.bfloat16

    def feature_row(y):
        return voxels[y].astype(jnp.float32) * occupancy[pl.ds(y, 1), :].astype(jnp.float32)

    def piece(bb, aa):
        return bb * m + aa + bb * (m - 1 - 2 * aa)

    def owner(j):
        bb = j // m
        aa = j % m
        return (aa + bb * (m - 1 - 2 * aa)) * 2 + bb

    def span(j):
        return pl.ds(j * rows, rows)

    barrier = pltpu.get_barrier_semaphore()
    for step in range(1, 2 * n):
        spot = (me * 2 + g + step) % (2 * n)
        pl.semaphore_signal(barrier, inc=1, device_id={"gx": spot // 2, "gy": spot % 2}, device_id_type=MESH)

    rw = jnp.broadcast_to(row_weights[...].astype(jnp.float32), (chans, chans))
    rw = jnp.sum(rw * identity(chans), axis=1, keepdims=True)
    group = 4 if rows % 4 == 0 else 2

    def yz_terms(step, carry):
        for k in range(group):
            y = step * group + k
            part[y] = (feature_row(y) * rw).astype(bf)
        return carry

    lax.fori_loop(0, count // group, yz_terms, 0)
    turned[...] = flipped(column_weights[...])
    wide[...] = flipped(expand[...]).astype(bf)
    for p in range(plane_kernels.shape[0]):
        for layer in range(2):
            for off in range(3):
                taps = plane_kernels[p, layer, :, off].reshape(3 * chans, chans)
                weights[p, layer, off * chans : (off + 1) * chans, :] = flipped(taps).astype(bf)
    pl.semaphore_wait(barrier, 2 * n - 1)

    row_copies = []
    for dx in range(-reach, reach + 1):
        for dg in range(2):
            if dx == 0 and dg == 0:
                continue
            slot = reach - dx
            copy = pltpu.make_async_remote_copy(
                src_ref=rows_in,
                dst_ref=row_slots.at[slot, dg],
                send_sem=row_s.at[slot, dg],
                recv_sem=row_r.at[slot, dg],
                device_id={"gx": jnp.clip(me + dx, 0, n - 1), "gy": (g + dg) % 2},
                device_id_type=MESH,
            )
            row_copies.append((dx, copy))

    order = list(range(1, m)) + [0]
    pair_copies = []
    for t, off in enumerate(order):
        aa = (a + off) % m
        pair_copies.append(
            pltpu.make_async_remote_copy(
                src_ref=part.at[span(piece(1 - b, aa))],
                dst_ref=pair_in.at[t],
                send_sem=pair_s.at[t],
                recv_sem=pair_r.at[t],
                device_id={"gx": a * 2 + 1 - b},
                device_id_type=MESH,
            )
        )
    for copy in pair_copies:
        copy.start()

    row_sums[...] = jnp.zeros(row_sums.shape, jnp.float32)
    depth = depth_weights[...].astype(jnp.float32)
    lane = lax.broadcasted_iota(jnp.int32, (chans, cols), 1)

    def row_terms(step, carry):
        xy, xz = row_sums[0], row_sums[1]
        for k in range(group):
            y = step * group + k
            f = feature_row(y)
            xy = jnp.where(lane == g * count + y, jnp.sum(f * depth, axis=1, keepdims=True), xy)
            xz = xz + f * column(turned[...], y)
        row_sums[0] = xy
        row_sums[1] = xz
        return carry

    lax.fori_loop(0, count // group, row_terms, 0)
    rows_in[...] = row_sums[...].astype(bf)
    for dx, copy in row_copies:
        pl.when((me + dx >= 0) & (me + dx < n))(copy.start)

    line_copies = []
    for t, off in enumerate(order[:-1]):
        aa = (a + off) % m
        pair_copies[t].wait_recv()
        mine = part[span(piece(b, aa))].astype(jnp.float32)
        pair_sum[t] = (mine + pair_in[t].astype(jnp.float32)).astype(jnp.bfloat16)
        copy = pltpu.make_async_remote_copy(
            src_ref=pair_sum.at[t],
            dst_ref=line_in.at[t],
            send_sem=line_s.at[t],
            recv_sem=line_r.at[t],
            device_id={"gx": aa * 2 + b},
            device_id_type=MESH,
        )
        copy.start()
        line_copies.append(copy)

    for dx, copy in row_copies:
        pl.when((me - dx >= 0) & (me - dx < n))(copy.wait_recv)
    planes = rows_in.shape[0]
    for s in range(2 * reach + 1):
        at = me + s - reach
        inside = (at >= 0) & (at < n)
        here = pl.ds(s * chans, chans)

        @pl.when(inside)
        def _():
            first = rows_in[...] if s == reach else row_slots[s, 0]
            total = first.astype(jnp.float32) + row_slots[s, 1].astype(jnp.float32)
            row_plane[:, here, :] = total.astype(jnp.bfloat16)

        @pl.when(jnp.logical_not(inside))
        def _():
            row_plane[:, here, :] = jnp.zeros((planes, chans, cols), jnp.bfloat16)

    for p in range(planes):
        for s in range(3):
            at = me + s - 1
            keep = ((at >= 0) & (at < n)).astype(jnp.float32)
            inner = silu(conv_row(row_plane[p, s * chans : (s + 3) * chans, :], weights[p, 0]))
            row_inner[p, s * chans : (s + 1) * chans, :] = (inner * keep).astype(jnp.bfloat16)
    xy_out[...] = conv_row(row_inner[0], weights[0, 1]).astype(bf).astype(jnp.float32)
    xz_out[...] = conv_row(row_inner[1], weights[1, 1]).astype(bf).astype(jnp.float32)

    mine_at = piece(b, a)
    pair_copies[m - 1].wait_recv()
    for copy in line_copies:
        copy.wait_recv()
    total = part[span(mine_at)].astype(jnp.float32) + pair_in[m - 1].astype(jnp.float32)
    for t in range(m - 1):
        total = total + line_in[t].astype(jnp.float32)
    yz_plane[pl.ds(reach * chans, rows * chans), :] = total.astype(jnp.bfloat16).reshape(rows * chans, cols)

    place = g * n + mine_at
    last = 2 * n - 1
    edge = reach * chans
    before = jnp.maximum(place - 1, 0)
    after = jnp.minimum(place + 1, last)
    up = pltpu.make_async_remote_copy(
        src_ref=yz_plane.at[pl.ds(edge, edge)],
        dst_ref=yz_plane.at[pl.ds(edge + rows * chans, edge)],
        send_sem=halo_s.at[0],
        recv_sem=halo_r.at[0],
        device_id={"gx": owner(before % n), "gy": before // n},
        device_id_type=MESH,
    )
    down = pltpu.make_async_remote_copy(
        src_ref=yz_plane.at[pl.ds(rows * chans, edge)],
        dst_ref=yz_plane.at[pl.ds(0, edge)],
        send_sem=halo_s.at[1],
        recv_sem=halo_r.at[1],
        device_id={"gx": owner(after % n), "gy": after // n},
        device_id_type=MESH,
    )
    pl.when(place > 0)(up.start)
    pl.when(place < last)(down.start)

    @pl.when(place == 0)
    def _():
        yz_plane[pl.ds(0, edge), :] = jnp.zeros((edge, cols), jnp.bfloat16)

    @pl.when(place == last)
    def _():
        yz_plane[pl.ds(edge + rows * chans, edge), :] = jnp.zeros((edge, cols), jnp.bfloat16)

    def inner_row(i, keep):
        window = yz_plane[pl.ds(pl.multiple_of(i * chans, chans), 3 * chans), :]
        inner = silu(conv_row(window, weights[2, 0])) * keep
        yz_inner[pl.ds(pl.multiple_of(i * chans, chans), chans), :] = inner.astype(jnp.bfloat16)

    for i in range(reach, rows):
        inner_row(i, 1.0)
    pl.when(place < last)(up.wait_recv)
    pl.when(place > 0)(down.wait_recv)
    for i in list(range(reach)) + list(range(rows, rows + 2)):
        keep = 1.0
        if i == 0:
            keep = (place > 0).astype(jnp.float32)
        if i == rows + 1:
            keep = (place < last).astype(jnp.float32)
        inner_row(i, keep)
    for r in range(rows):
        done = conv_row(yz_inner[pl.ds(r * chans, 3 * chans), :], weights[2, 1])
        yz_out[mine_at * rows + r] = done.astype(jnp.bfloat16)

    def give(j, send, recv, target):
        return pltpu.make_async_remote_copy(
            src_ref=yz_out.at[span(j)],
            dst_ref=yz_out.at[span(j)],
            send_sem=send,
            recv_sem=recv,
            device_id={"gx": target},
            device_id_type=MESH,
        )

    def finish(j):
        def some_rows(step, carry):
            at = [j * rows + step * group + k for k in range(group)]
            mixed = []
            for y in at:
                product = column(xy_out[...], g * count + y) * xz_out[...]
                product = product * yz_out[y].astype(jnp.float32)
                mixed.append((product_scale * product).astype(bf))
            mixed = jnp.concatenate(mixed, axis=1)
            hidden = silu(jnp.dot(wide[...], mixed, preferred_element_type=jnp.float32)).astype(bf)
            branch = jnp.dot(shrink[...], hidden, preferred_element_type=jnp.float32)
            for k, y in enumerate(at):
                updated[y] = (feature_row(y) + branch[:, k * cols : (k + 1) * cols]).astype(bf)
            return carry

        lax.fori_loop(0, rows // group, some_rows, 0)

    partner = a * 2 + 1 - b
    sends = []
    for t in range(1, m):
        copy = give(mine_at, spread_s.at[t], spread_r.at[t], ((a + t) % m) * 2 + b)
        copy.start()
        sends.append(copy)
    copy = give(mine_at, cross_s.at[0], cross_r.at[0], partner)
    copy.start()
    sends.append(copy)
    finish(mine_at)
    for t in range(1, m):
        j = piece(b, (a + m - t) % m)
        give(j, spread_s.at[t], spread_r.at[t], partner).wait_recv()
        copy = give(j, cross_s.at[t], cross_r.at[t], partner)
        copy.start()
        sends.append(copy)
        finish(j)
    for t in range(m):
        j = piece(1 - b, (a + m - t) % m)
        give(j, cross_s.at[t], cross_r.at[t], partner).wait_recv()
        finish(j)
    for copy in sends + pair_copies + line_copies:
        copy.wait_send()
    for dx, copy in row_copies:
        pl.when((me + dx >= 0) & (me + dx < n))(copy.wait_send)
    pl.when(place > 0)(up.wait_send)
    pl.when(place < last)(down.wait_send)


def fused(voxels, occupancy, row_weights, column_weights, depth_weights, plane_kernels, expand_weight, shrink_weight):
    n = lax.axis_size("gx")
    m = n // 2
    count, cols, chans = voxels.shape[1:]
    rows = count // n
    sets, layers = plane_kernels.shape[:2]
    planes = 2
    span = 2 * reach + 1
    bf = jnp.bfloat16
    f32 = jnp.float32
    dma = pltpu.SemaphoreType.DMA
    updated = pl.pallas_call(
        functools.partial(block_kernel, n),
        out_shape=jax.ShapeDtypeStruct((count, chans, cols), bf),
        in_specs=[pl.BlockSpec(memory_space=pltpu.VMEM)] * 8,
        out_specs=pl.BlockSpec(memory_space=pltpu.VMEM),
        scratch_shapes=[
            pltpu.VMEM((count, chans, cols), bf),
            pltpu.VMEM((planes, chans, cols), bf),
            pltpu.VMEM((sets, layers, 3 * chans, 3 * chans), bf),
            pltpu.VMEM(expand_weight.shape[::-1], bf),
            pltpu.VMEM((count, chans, cols), bf),
            pltpu.VMEM((chans, 2 * count), f32),
            pltpu.VMEM((chans, cols), f32),
            pltpu.VMEM((planes, chans, cols), f32),
            pltpu.VMEM((chans, count), f32),
            pltpu.VMEM((m, rows, chans, cols), bf),
            pltpu.VMEM((m, rows, chans, cols), bf),
            pltpu.VMEM((m, rows, chans, cols), bf),
            pltpu.VMEM(((rows + 4) * chans, cols), bf),
            pltpu.VMEM(((rows + 2) * chans, cols), bf),
            pltpu.VMEM((span, 2, planes, chans, cols), bf),
            pltpu.VMEM((planes, span * chans, cols), bf),
            pltpu.VMEM((planes, 3 * chans, cols), bf),
            dma((m,)), dma((m,)), dma((m,)), dma((m,)), dma((2,)), dma((2,)),
            dma((span, 2)), dma((span, 2)), dma((m,)), dma((m,)), dma((m,)), dma((m,)),
        ],
        compiler_params=pltpu.CompilerParams(collective_id=0, has_side_effects=True),
    )(
        voxels[0].transpose(0, 2, 1),
        occupancy[0],
        row_weights,
        column_weights,
        depth_weights.T,
        plane_kernels,
        expand_weight,
        shrink_weight.T,
    )
    return updated.transpose(0, 2, 1)[None]


def fits(voxels):
    n = lax.axis_size("gx")
    sides = lax.axis_size("gy")
    xs, ys, zs, _ = voxels.shape
    return xs == 1 and sides == 2 and n % 2 == 0 and n >= 4 and ys % n == 0 and ys // n >= reach and ys // n % 2 == 0 and 2 * ys == zs


def plain_planes(features, row_weights, column_weights, depth_weights, plane_kernels):
    xy_plane = jnp.einsum(
        "xyzc,zc->xyc", features, depth_weights, preferred_element_type=jnp.float32
    ).astype(jnp.bfloat16)
    xz_part = jnp.einsum(
        "xyzc,yc->xzc", features, column_weights, preferred_element_type=jnp.float32
    )
    yz_part = jnp.einsum("xyzc,xc->yzc", features, row_weights, preferred_element_type=jnp.float32)
    xy_out = plane_block(xy_plane, plane_kernels[0], rim_xy)
    xz_plane = lax.psum(xz_part, "gy").astype(jnp.bfloat16)
    xz_out = plane_block(xz_plane, plane_kernels[1], rim_xz)
    yz_plane = lax.psum(yz_part, "gx").astype(jnp.bfloat16)
    yz_out = plane_block(yz_plane, plane_kernels[2], rim_yz)
    return xy_out, xz_out, yz_out


def shards(
    voxels,
    occupancy,
    row_weights,
    column_weights,
    depth_weights,
    plane_kernels,
    expand_weight,
    shrink_weight,
):
    if fits(voxels):
        return fused(
            voxels,
            occupancy,
            row_weights,
            column_weights,
            depth_weights,
            plane_kernels,
            expand_weight,
            shrink_weight,
        )
    features = voxels * occupancy.astype(jnp.bfloat16)[..., None]
    xy_out, xz_out, yz_out = plain_planes(features, row_weights, column_weights, depth_weights, plane_kernels)
    product = xy_out.astype(jnp.float32)[:, :, None, :] * xz_out.astype(jnp.float32)[:, None, :, :]
    product = product * yz_out.astype(jnp.float32)[None, :, :, :]
    mixed = (product_scale * product).astype(jnp.bfloat16)
    hidden = jax.nn.silu(
        jnp.einsum("xyzc,ch->xyzh", mixed, expand_weight, preferred_element_type=jnp.float32)
    ).astype(jnp.bfloat16)
    branch = jnp.einsum("xyzh,hc->xyzc", hidden, shrink_weight, preferred_element_type=jnp.float32)
    return (features.astype(jnp.float32) + branch).astype(jnp.bfloat16)


def solution(mesh):
    in_specs = (
        P(("groups", "gx"), "gy", None, None),
        P(("groups", "gx"), "gy", None),
        P("gx", None),
        P("gy", None),
        P(),
        P(),
        P(),
        P(),
    )
    out_specs = P(("groups", "gx"), "gy", None, None)
    return jax.shard_map(shards, mesh=mesh, in_specs=in_specs, out_specs=out_specs, check_vma=False)
```

```python
import functools

import jax
import jax.numpy as jnp
from jax import lax
from jax.experimental import pallas as pl
from jax.experimental.pallas import tpu as pltpu
from jax.sharding import PartitionSpec as P

MESH = pl.DeviceIdType.MESH
reach = 2
cuts = 2

product_scale = 8.0


def with_halo(cells, sides, width):
    for axis, dim in sides:
        count = lax.axis_size(axis)
        ends = count - 1
        head = lax.slice_in_dim(cells, 0, width, axis=dim)
        tail = lax.slice_in_dim(cells, cells.shape[dim] - width, cells.shape[dim], axis=dim)
        cells = jnp.concatenate(
            [
                lax.ppermute(tail, axis, [(i, (i + 1) % count) for i in range(ends)]),
                cells,
                lax.ppermute(head, axis, [((i + 1) % count, i) for i in range(ends)]),
            ],
            axis=dim,
        )
    return cells


def conv_valid(padded, kernel):
    rows = padded.shape[0] - 2
    cols = padded.shape[1] - 2
    total = jnp.zeros((rows, cols, kernel.shape[-1]), jnp.float32)
    for row_off in range(3):
        for col_off in range(3):
            window = padded[row_off : row_off + rows, col_off : col_off + cols]
            total = total + jnp.einsum(
                "ijc,co->ijo", window, kernel[row_off, col_off], preferred_element_type=jnp.float32
            )
    return total


def plane_block(plane, kernels, extend):
    inner = jax.nn.silu(conv_valid(extend(plane), kernels[0])).astype(jnp.bfloat16)
    return conv_valid(extend(inner), kernels[1]).astype(jnp.bfloat16)


def rim_xy(plane):
    return with_halo(plane, (("gx", 0), ("gy", 1)), 1)


def rim_xz(plane):
    padded = with_halo(plane, (("gx", 0),), 1)
    return jnp.pad(padded, ((0, 0), (1, 1), (0, 0)))


def rim_yz(plane):
    padded = with_halo(plane, (("gy", 0),), 1)
    return jnp.pad(padded, ((0, 0), (1, 1), (0, 0)))


def conv_row(window, weight):
    taps = jnp.dot(weight, window, preferred_element_type=jnp.float32)
    chans = taps.shape[0] // 3
    cols = taps.shape[1]
    lane = lax.broadcasted_iota(jnp.int32, (chans, cols), 1)
    left = pltpu.roll(taps[:chans], 1, 1)
    right = pltpu.roll(taps[2 * chans :], cols - 1, 1)
    left = jnp.where(lane == 0, 0.0, left)
    right = jnp.where(lane == cols - 1, 0.0, right)
    return taps[chans : 2 * chans] + left + right


def silu(v):
    return v / (1.0 + jnp.exp(-v))


def identity(size):
    row = lax.broadcasted_iota(jnp.int32, (size, size), 0)
    col = lax.broadcasted_iota(jnp.int32, (size, size), 1)
    return jnp.where(row == col, 1.0, 0.0)


def flipped(x):
    eye = identity(x.shape[1]).astype(x.dtype)
    return lax.dot_general(eye, x, (((1,), (1,)), ((), ())), preferred_element_type=jnp.float32)


def column(x, at):
    lane = lax.broadcasted_iota(jnp.int32, x.shape, 1)
    return jnp.sum(jnp.where(lane == at, x, 0.0), axis=1, keepdims=True)


def block_kernel(
    n, voxels, occupancy, row_weights, column_weights, depth_weights, plane_kernels, expand, shrink, updated,
    part, rows_in, weights, wide, yz_out, xy_out, xz_out, row_sums, turned,
    pair_in, pair_sum, line_in, yz_sum, yz_plane, yz_inner, row_slots, row_plane, row_inner,
    pair_s, pair_r, line_s, line_r, halo_s, halo_r, row_s, row_r, spread_s, spread_r, cross_s, cross_r,
):
    me = lax.axis_index("gx")
    g = lax.axis_index("gy")
    m = n // 2
    a = me // 2
    b = me % 2
    count, chans, cols = part.shape
    rows = count // n
    bf = jnp.bfloat16

    def feature_row(y):
        return voxels[y].astype(jnp.float32) * occupancy[pl.ds(y, 1), :].astype(jnp.float32)

    def piece(bb, aa):
        return bb * m + aa + bb * (m - 1 - 2 * aa)

    def owner(j):
        bb = j // m
        aa = j % m
        return (aa + bb * (m - 1 - 2 * aa)) * 2 + bb

    def span(j):
        return pl.ds(j * rows, rows)

    barrier = pltpu.get_barrier_semaphore()
    for step in range(1, 2 * n):
        spot = (me * 2 + g + step) % (2 * n)
        pl.semaphore_signal(barrier, inc=1, device_id={"gx": spot // 2, "gy": spot % 2}, device_id_type=MESH)

    rw = jnp.broadcast_to(row_weights[...].astype(jnp.float32), (chans, chans))
    rw = jnp.sum(rw * identity(chans), axis=1, keepdims=True)
    group = 4 if rows % 4 == 0 else 2

    def yz_terms(step, carry):
        for k in range(group):
            y = step * group + k
            part[y] = (feature_row(y) * rw).astype(bf)
        return carry

    lax.fori_loop(0, count // group, yz_terms, 0)
    pl.semaphore_wait(barrier, 2 * n - 1)

    row_copies = []
    for dx in range(-reach, reach + 1):
        for dg in range(2):
            if dx == 0 and dg == 0:
                continue
            slot = reach - dx
            copy = pltpu.make_async_remote_copy(
                src_ref=rows_in,
                dst_ref=row_slots.at[slot, dg],
                send_sem=row_s.at[slot, dg],
                recv_sem=row_r.at[slot, dg],
                device_id={"gx": jnp.clip(me + dx, 0, n - 1), "gy": (g + dg) % 2},
                device_id_type=MESH,
            )
            row_copies.append((dx, copy))

    sub = rows // cuts
    far = sorted([d for d in range(1 - m, m) if d != 0], key=lambda d: -abs(d))
    near = far[::-1]
    partner = a * 2 + 1 - b

    def valid(d):
        return (a + d >= 0) & (a + d < m)

    def spot(d):
        return jnp.clip(a + d, 0, m - 1)

    def sub_span(j, h):
        return pl.ds(j * rows + h * sub, sub)

    pair_copies = {}
    line_copies = {}
    for d in far + [0]:
        for h in range(cuts):
            pair_copies[d, h] = pltpu.make_async_remote_copy(
                src_ref=part.at[sub_span(piece(1 - b, spot(d)), h)],
                dst_ref=pair_in.at[d + m - 1, h],
                send_sem=pair_s.at[d + m - 1, h],
                recv_sem=pair_r.at[d + m - 1, h],
                device_id={"gx": partner},
                device_id_type=MESH,
            )
            if d != 0:
                line_copies[d, h] = pltpu.make_async_remote_copy(
                    src_ref=pair_sum.at[d + m - 1, h],
                    dst_ref=line_in.at[d + m - 1, h],
                    send_sem=line_s.at[d + m - 1, h],
                    recv_sem=line_r.at[d + m - 1, h],
                    device_id={"gx": spot(d) * 2 + b},
                    device_id_type=MESH,
                )
    for (d, h), copy in pair_copies.items():
        pl.when(valid(d))(copy.start)
    for d in far:
        for h in range(cuts):

            @pl.when(valid(d))
            def _():
                pair_copies[d, h].wait_recv()
                mine = part[sub_span(piece(b, spot(d)), h)].astype(jnp.float32)
                pair_sum[d + m - 1, h] = (mine + pair_in[d + m - 1, h].astype(jnp.float32)).astype(bf)
                line_copies[d, h].start()

    turned[...] = flipped(column_weights[...])
    wide[...] = flipped(expand[...]).astype(bf)
    for p in range(plane_kernels.shape[0]):
        for layer in range(2):
            for off in range(3):
                taps = plane_kernels[p, layer, :, off].reshape(3 * chans, chans)
                weights[p, layer, off * chans : (off + 1) * chans, :] = flipped(taps).astype(bf)

    row_sums[...] = jnp.zeros(row_sums.shape, jnp.float32)
    depth = depth_weights[...].astype(jnp.float32)
    lane = lax.broadcasted_iota(jnp.int32, (chans, cols), 1)

    def row_terms(step, carry):
        xy, xz = row_sums[0], row_sums[1]
        for k in range(group):
            y = step * group + k
            f = feature_row(y)
            xy = jnp.where(lane == g * count + y, jnp.sum(f * depth, axis=1, keepdims=True), xy)
            xz = xz + f * column(turned[...], y)
        row_sums[0] = xy
        row_sums[1] = xz
        return carry

    lax.fori_loop(0, count // group, row_terms, 0)
    rows_in[...] = row_sums[...].astype(bf)
    mine_at = piece(b, a)
    for h in range(cuts):
        at = pl.ds(h * sub, sub)
        pair_copies[0, h].wait_recv()
        mine = part[sub_span(mine_at, h)].astype(jnp.float32)
        yz_sum[at] = mine + pair_in[m - 1, h].astype(jnp.float32)
    for d in near:
        for h in range(cuts):

            @pl.when(valid(-d))
            def _():
                at = pl.ds(h * sub, sub)
                line_copies[d, h].wait_recv()
                yz_sum[at] = yz_sum[at] + line_in[d + m - 1, h].astype(jnp.float32)

    yz_plane[pl.ds(reach * chans, rows * chans), :] = yz_sum[...].astype(bf).reshape(rows * chans, cols)

    place = g * n + mine_at
    last = 2 * n - 1
    edge = reach * chans
    before = jnp.maximum(place - 1, 0)
    after = jnp.minimum(place + 1, last)
    up = pltpu.make_async_remote_copy(
        src_ref=yz_plane.at[pl.ds(edge, edge)],
        dst_ref=yz_plane.at[pl.ds(edge + rows * chans, edge)],
        send_sem=halo_s.at[0],
        recv_sem=halo_r.at[0],
        device_id={"gx": owner(before % n), "gy": before // n},
        device_id_type=MESH,
    )
    down = pltpu.make_async_remote_copy(
        src_ref=yz_plane.at[pl.ds(rows * chans, edge)],
        dst_ref=yz_plane.at[pl.ds(0, edge)],
        send_sem=halo_s.at[1],
        recv_sem=halo_r.at[1],
        device_id={"gx": owner(after % n), "gy": after // n},
        device_id_type=MESH,
    )
    pl.when(place > 0)(up.start)
    pl.when(place < last)(down.start)
    for dx, copy in row_copies:
        pl.when((me + dx >= 0) & (me + dx < n))(copy.start)

    @pl.when(place == 0)
    def _():
        yz_plane[pl.ds(0, edge), :] = jnp.zeros((edge, cols), jnp.bfloat16)

    @pl.when(place == last)
    def _():
        yz_plane[pl.ds(edge + rows * chans, edge), :] = jnp.zeros((edge, cols), jnp.bfloat16)

    def inner_row(i, keep):
        window = yz_plane[pl.ds(pl.multiple_of(i * chans, chans), 3 * chans), :]
        inner = silu(conv_row(window, weights[2, 0])) * keep
        yz_inner[pl.ds(pl.multiple_of(i * chans, chans), chans), :] = inner.astype(jnp.bfloat16)

    for i in range(reach, rows):
        inner_row(i, 1.0)
    pl.when(place < last)(up.wait_recv)
    pl.when(place > 0)(down.wait_recv)
    for i in list(range(reach)) + list(range(rows, rows + 2)):
        keep = 1.0
        if i == 0:
            keep = (place > 0).astype(jnp.float32)
        if i == rows + 1:
            keep = (place < last).astype(jnp.float32)
        inner_row(i, keep)
    def give(j, h, sems, at, target):
        return pltpu.make_async_remote_copy(
            src_ref=yz_out.at[sub_span(j, h)],
            dst_ref=yz_out.at[sub_span(j, h)],
            send_sem=sems[0].at[at, h],
            recv_sem=sems[1].at[at, h],
            device_id={"gx": target},
            device_id_type=MESH,
        )

    spread = (spread_s, spread_r)
    cross = (cross_s, cross_r)
    sends = []
    for h in range(cuts):
        for r in range(h * sub, (h + 1) * sub):
            done = conv_row(yz_inner[pl.ds(r * chans, 3 * chans), :], weights[2, 1])
            yz_out[mine_at * rows + r] = done.astype(bf)
        for d in far:
            copy = give(mine_at, h, spread, d + m - 1, spot(d) * 2 + b)
            pl.when(valid(d))(copy.start)
            sends.append((d, copy))
        copy = give(mine_at, h, cross, m - 1, partner)
        copy.start()
        sends.append((0, copy))

    for dx, copy in row_copies:
        pl.when((me - dx >= 0) & (me - dx < n))(copy.wait_recv)
    planes = rows_in.shape[0]
    for s in range(2 * reach + 1):
        at = me + s - reach
        inside = (at >= 0) & (at < n)
        here = pl.ds(s * chans, chans)

        @pl.when(inside)
        def _():
            first = rows_in[...] if s == reach else row_slots[s, 0]
            total = first.astype(jnp.float32) + row_slots[s, 1].astype(jnp.float32)
            row_plane[:, here, :] = total.astype(jnp.bfloat16)

        @pl.when(jnp.logical_not(inside))
        def _():
            row_plane[:, here, :] = jnp.zeros((planes, chans, cols), jnp.bfloat16)

    for p in range(planes):
        for s in range(3):
            at = me + s - 1
            keep = ((at >= 0) & (at < n)).astype(jnp.float32)
            inner = silu(conv_row(row_plane[p, s * chans : (s + 3) * chans, :], weights[p, 0]))
            row_inner[p, s * chans : (s + 1) * chans, :] = (inner * keep).astype(jnp.bfloat16)
    xy_out[...] = conv_row(row_inner[0], weights[0, 1]).astype(bf).astype(jnp.float32)
    xz_out[...] = conv_row(row_inner[1], weights[1, 1]).astype(bf).astype(jnp.float32)

    step_rows = 4 if sub % 4 == 0 else (2 if sub % 2 == 0 else 1)

    def finish(j, h):
        def some_rows(step, carry):
            at = [j * rows + h * sub + step * step_rows + k for k in range(step_rows)]
            mixed = []
            for y in at:
                product = column(xy_out[...], g * count + y) * xz_out[...]
                product = product * yz_out[y].astype(jnp.float32)
                mixed.append((product_scale * product).astype(bf))
            mixed = jnp.concatenate(mixed, axis=1)
            hidden = silu(jnp.dot(wide[...], mixed, preferred_element_type=jnp.float32)).astype(bf)
            branch = jnp.dot(shrink[...], hidden, preferred_element_type=jnp.float32)
            for k, y in enumerate(at):
                updated[y] = (feature_row(y) + branch[:, k * cols : (k + 1) * cols]).astype(bf)
            return carry

        lax.fori_loop(0, sub // step_rows, some_rows, 0)

    for h in range(cuts):
        finish(mine_at, h)
    for d in near:
        for h in range(cuts):

            @pl.when(valid(d))
            def _():
                j = piece(b, spot(d))
                give(j, h, spread, m - 1 - d, partner).wait_recv()
                give(j, h, cross, m - 1 + d, partner).start()
                finish(j, h)

    for d in [0] + near:
        for h in range(cuts):

            @pl.when(valid(d))
            def _():
                j = piece(1 - b, spot(d))
                give(j, h, cross, m - 1 + d, partner).wait_recv()
                finish(j, h)

    for d in near:
        for h in range(cuts):
            pl.when(valid(d))(give(piece(b, spot(d)), h, cross, m - 1 + d, partner).wait_send)
    for d, copy in sends:
        pl.when(valid(d))(copy.wait_send)
    for (d, h), copy in list(pair_copies.items()) + list(line_copies.items()):
        pl.when(valid(d))(copy.wait_send)
    for dx, copy in row_copies:
        pl.when((me + dx >= 0) & (me + dx < n))(copy.wait_send)
    pl.when(place > 0)(up.wait_send)
    pl.when(place < last)(down.wait_send)


def fused(voxels, occupancy, row_weights, column_weights, depth_weights, plane_kernels, expand_weight, shrink_weight):
    n = lax.axis_size("gx")
    m = n // 2
    count, cols, chans = voxels.shape[1:]
    rows = count // n
    sets, layers = plane_kernels.shape[:2]
    planes = 2
    span = 2 * reach + 1
    bf = jnp.bfloat16
    f32 = jnp.float32
    dma = pltpu.SemaphoreType.DMA
    block = dma((2 * m - 1, cuts))
    updated = pl.pallas_call(
        functools.partial(block_kernel, n),
        out_shape=pltpu.VMEM((count, chans, cols), bf),
        in_specs=[pl.BlockSpec(memory_space=pltpu.VMEM)] * 8,
        out_specs=pl.BlockSpec(memory_space=pltpu.VMEM),
        scratch_shapes=[
            pltpu.VMEM((count, chans, cols), bf),
            pltpu.VMEM((planes, chans, cols), bf),
            pltpu.VMEM((sets, layers, 3 * chans, 3 * chans), bf),
            pltpu.VMEM(expand_weight.shape[::-1], bf),
            pltpu.VMEM((count, chans, cols), bf),
            pltpu.VMEM((chans, 2 * count), f32),
            pltpu.VMEM((chans, cols), f32),
            pltpu.VMEM((planes, chans, cols), f32),
            pltpu.VMEM((chans, count), f32),
            pltpu.VMEM((2 * m - 1, cuts, rows // cuts, chans, cols), bf),
            pltpu.VMEM((2 * m - 1, cuts, rows // cuts, chans, cols), bf),
            pltpu.VMEM((2 * m - 1, cuts, rows // cuts, chans, cols), bf),
            pltpu.VMEM((rows, chans, cols), f32),
            pltpu.VMEM(((rows + 4) * chans, cols), bf),
            pltpu.VMEM(((rows + 2) * chans, cols), bf),
            pltpu.VMEM((span, 2, planes, chans, cols), bf),
            pltpu.VMEM((planes, span * chans, cols), bf),
            pltpu.VMEM((planes, 3 * chans, cols), bf),
            block, block, block, block, dma((2,)), dma((2,)),
            dma((span, 2)), dma((span, 2)), block, block, block, block,
        ],
        compiler_params=pltpu.CompilerParams(collective_id=0, has_side_effects=True),
    )(
        voxels[0].transpose(0, 2, 1),
        occupancy[0],
        row_weights,
        column_weights,
        depth_weights.T,
        plane_kernels,
        expand_weight,
        shrink_weight.T,
    )
    return updated.transpose(0, 2, 1)[None]


def fits(voxels):
    n = lax.axis_size("gx")
    sides = lax.axis_size("gy")
    xs, ys, zs, _ = voxels.shape
    return xs == 1 and sides == 2 and n % 2 == 0 and n >= 4 and ys % n == 0 and ys // n >= reach and ys // n % cuts == 0 and 2 * ys == zs


def plain_planes(features, row_weights, column_weights, depth_weights, plane_kernels):
    xy_plane = jnp.einsum(
        "xyzc,zc->xyc", features, depth_weights, preferred_element_type=jnp.float32
    ).astype(jnp.bfloat16)
    xz_part = jnp.einsum(
        "xyzc,yc->xzc", features, column_weights, preferred_element_type=jnp.float32
    )
    yz_part = jnp.einsum("xyzc,xc->yzc", features, row_weights, preferred_element_type=jnp.float32)
    xy_out = plane_block(xy_plane, plane_kernels[0], rim_xy)
    xz_plane = lax.psum(xz_part, "gy").astype(jnp.bfloat16)
    xz_out = plane_block(xz_plane, plane_kernels[1], rim_xz)
    yz_plane = lax.psum(yz_part, "gx").astype(jnp.bfloat16)
    yz_out = plane_block(yz_plane, plane_kernels[2], rim_yz)
    return xy_out, xz_out, yz_out


def shards(
    voxels,
    occupancy,
    row_weights,
    column_weights,
    depth_weights,
    plane_kernels,
    expand_weight,
    shrink_weight,
):
    if fits(voxels):
        return fused(
            voxels,
            occupancy,
            row_weights,
            column_weights,
            depth_weights,
            plane_kernels,
            expand_weight,
            shrink_weight,
        )
    features = voxels * occupancy.astype(jnp.bfloat16)[..., None]
    xy_out, xz_out, yz_out = plain_planes(features, row_weights, column_weights, depth_weights, plane_kernels)
    product = xy_out.astype(jnp.float32)[:, :, None, :] * xz_out.astype(jnp.float32)[:, None, :, :]
    product = product * yz_out.astype(jnp.float32)[None, :, :, :]
    mixed = (product_scale * product).astype(jnp.bfloat16)
    hidden = jax.nn.silu(
        jnp.einsum("xyzc,ch->xyzh", mixed, expand_weight, preferred_element_type=jnp.float32)
    ).astype(jnp.bfloat16)
    branch = jnp.einsum("xyzh,hc->xyzc", hidden, shrink_weight, preferred_element_type=jnp.float32)
    return (features.astype(jnp.float32) + branch).astype(jnp.bfloat16)


def solution(mesh):
    in_specs = (
        P(("groups", "gx"), "gy", None, None),
        P(("groups", "gx"), "gy", None),
        P("gx", None),
        P("gy", None),
        P(),
        P(),
        P(),
        P(),
    )
    out_specs = P(("groups", "gx"), "gy", None, None)
    return jax.shard_map(shards, mesh=mesh, in_specs=in_specs, out_specs=out_specs, check_vma=False)
```

```python
import functools

import jax
import jax.numpy as jnp
from jax import lax
from jax.experimental import pallas as pl
from jax.experimental.pallas import tpu as pltpu
from jax.sharding import PartitionSpec as P

MESH = pl.DeviceIdType.MESH
reach = 2
cuts = 2

product_scale = 8.0


def with_halo(cells, sides, width):
    for axis, dim in sides:
        count = lax.axis_size(axis)
        ends = count - 1
        head = lax.slice_in_dim(cells, 0, width, axis=dim)
        tail = lax.slice_in_dim(cells, cells.shape[dim] - width, cells.shape[dim], axis=dim)
        cells = jnp.concatenate(
            [
                lax.ppermute(tail, axis, [(i, (i + 1) % count) for i in range(ends)]),
                cells,
                lax.ppermute(head, axis, [((i + 1) % count, i) for i in range(ends)]),
            ],
            axis=dim,
        )
    return cells


def conv_valid(padded, kernel):
    rows = padded.shape[0] - 2
    cols = padded.shape[1] - 2
    total = jnp.zeros((rows, cols, kernel.shape[-1]), jnp.float32)
    for row_off in range(3):
        for col_off in range(3):
            window = padded[row_off : row_off + rows, col_off : col_off + cols]
            total = total + jnp.einsum(
                "ijc,co->ijo", window, kernel[row_off, col_off], preferred_element_type=jnp.float32
            )
    return total


def plane_block(plane, kernels, extend):
    inner = jax.nn.silu(conv_valid(extend(plane), kernels[0])).astype(jnp.bfloat16)
    return conv_valid(extend(inner), kernels[1]).astype(jnp.bfloat16)


def rim_xy(plane):
    return with_halo(plane, (("gx", 0), ("gy", 1)), 1)


def rim_xz(plane):
    padded = with_halo(plane, (("gx", 0),), 1)
    return jnp.pad(padded, ((0, 0), (1, 1), (0, 0)))


def rim_yz(plane):
    padded = with_halo(plane, (("gy", 0),), 1)
    return jnp.pad(padded, ((0, 0), (1, 1), (0, 0)))


def conv_row(window, weight):
    taps = jnp.dot(weight, window, preferred_element_type=jnp.float32)
    chans = taps.shape[0] // 3
    cols = taps.shape[1]
    lane = lax.broadcasted_iota(jnp.int32, (chans, cols), 1)
    left = pltpu.roll(taps[:chans], 1, 1)
    right = pltpu.roll(taps[2 * chans :], cols - 1, 1)
    left = jnp.where(lane == 0, 0.0, left)
    right = jnp.where(lane == cols - 1, 0.0, right)
    return taps[chans : 2 * chans] + left + right


def silu(v):
    return v / (1.0 + jnp.exp(-v))


def identity(size):
    row = lax.broadcasted_iota(jnp.int32, (size, size), 0)
    col = lax.broadcasted_iota(jnp.int32, (size, size), 1)
    return jnp.where(row == col, 1.0, 0.0)


def flipped(x):
    eye = identity(x.shape[1]).astype(x.dtype)
    return lax.dot_general(eye, x, (((1,), (1,)), ((), ())), preferred_element_type=jnp.float32)


def column(x, at):
    lane = lax.broadcasted_iota(jnp.int32, x.shape, 1)
    return jnp.sum(jnp.where(lane == at, x, 0.0), axis=1, keepdims=True)


def block_kernel(
    n, voxels, occupancy, row_weights, column_weights, depth_weights, plane_kernels, expand, shrink, updated,
    part, rows_in, weights, wide, yz_out, xy_out, xz_out, row_sums, turned,
    pair_in, pair_sum, line_in, yz_sum, yz_plane, yz_inner, row_slots, row_plane, row_inner,
    pair_s, pair_r, line_s, line_r, halo_s, halo_r, row_s, row_r, spread_s, spread_r, cross_s, cross_r,
):
    me = lax.axis_index("gx")
    g = lax.axis_index("gy")
    m = n // 2
    a = me // 2
    b = me % 2
    count, chans, cols = part.shape
    rows = count // n
    bf = jnp.bfloat16

    def feature_row(y):
        return voxels[y].astype(jnp.float32) * occupancy[pl.ds(y, 1), :].astype(jnp.float32)

    def piece(bb, aa):
        return bb * m + aa + bb * (m - 1 - 2 * aa)

    def owner(j):
        bb = j // m
        aa = j % m
        return (aa + bb * (m - 1 - 2 * aa)) * 2 + bb

    def span(j):
        return pl.ds(j * rows, rows)

    barrier = pltpu.get_barrier_semaphore()
    for step in range(1, 2 * n):
        spot = (me * 2 + g + step) % (2 * n)
        pl.semaphore_signal(barrier, inc=1, device_id={"gx": spot // 2, "gy": spot % 2}, device_id_type=MESH)

    rw = jnp.broadcast_to(row_weights[...].astype(jnp.float32), (chans, chans))
    rw = jnp.sum(rw * identity(chans), axis=1, keepdims=True)
    group = 4 if rows % 4 == 0 else 2

    def yz_terms(step, carry):
        for k in range(group):
            y = step * group + k
            part[y] = (feature_row(y) * rw).astype(bf)
        return carry

    lax.fori_loop(0, count // group, yz_terms, 0)
    pl.semaphore_wait(barrier, 2 * n - 1)

    row_copies = []
    for dx in range(-reach, reach + 1):
        for dg in range(2):
            if dx == 0 and dg == 0:
                continue
            slot = reach - dx
            copy = pltpu.make_async_remote_copy(
                src_ref=rows_in,
                dst_ref=row_slots.at[slot, dg],
                send_sem=row_s.at[slot, dg],
                recv_sem=row_r.at[slot, dg],
                device_id={"gx": jnp.clip(me + dx, 0, n - 1), "gy": (g + dg) % 2},
                device_id_type=MESH,
            )
            row_copies.append((dx, copy))

    sub = rows // cuts
    far = sorted([d for d in range(1 - m, m) if d != 0], key=lambda d: -abs(d))
    near = far[::-1]
    partner = a * 2 + 1 - b

    def valid(d):
        return (a + d >= 0) & (a + d < m)

    def spot(d):
        return jnp.clip(a + d, 0, m - 1)

    def sub_span(j, h):
        return pl.ds(j * rows + h * sub, sub)

    pair_copies = {}
    line_copies = {}
    for d in far + [0]:
        for h in range(cuts):
            pair_copies[d, h] = pltpu.make_async_remote_copy(
                src_ref=part.at[sub_span(piece(1 - b, spot(d)), h)],
                dst_ref=pair_in.at[d + m - 1, h],
                send_sem=pair_s.at[d + m - 1, h],
                recv_sem=pair_r.at[d + m - 1, h],
                device_id={"gx": partner},
                device_id_type=MESH,
            )
            if d != 0:
                line_copies[d, h] = pltpu.make_async_remote_copy(
                    src_ref=pair_sum.at[d + m - 1, h],
                    dst_ref=line_in.at[d + m - 1, h],
                    send_sem=line_s.at[d + m - 1, h],
                    recv_sem=line_r.at[d + m - 1, h],
                    device_id={"gx": spot(d) * 2 + b},
                    device_id_type=MESH,
                )
    for (d, h), copy in pair_copies.items():
        pl.when(valid(d))(copy.start)
    for d in far:
        for h in range(cuts):

            @pl.when(valid(d))
            def _():
                pair_copies[d, h].wait_recv()
                mine = part[sub_span(piece(b, spot(d)), h)].astype(jnp.float32)
                pair_sum[d + m - 1, h] = (mine + pair_in[d + m - 1, h].astype(jnp.float32)).astype(bf)
                line_copies[d, h].start()

    turned[...] = flipped(column_weights[...])
    wide[...] = flipped(expand[...]).astype(bf)
    for p in range(plane_kernels.shape[0]):
        for layer in range(2):
            for off in range(3):
                taps = plane_kernels[p, layer, :, off].reshape(3 * chans, chans)
                weights[p, layer, off * chans : (off + 1) * chans, :] = flipped(taps).astype(bf)

    row_sums[...] = jnp.zeros(row_sums.shape, jnp.float32)
    depth = depth_weights[...].astype(jnp.float32)
    lane = lax.broadcasted_iota(jnp.int32, (chans, cols), 1)

    def row_terms(step, carry):
        xy, xz = row_sums[0], row_sums[1]
        for k in range(group):
            y = step * group + k
            f = feature_row(y)
            xy = jnp.where(lane == g * count + y, jnp.sum(f * depth, axis=1, keepdims=True), xy)
            xz = xz + f * column(turned[...], y)
        row_sums[0] = xy
        row_sums[1] = xz
        return carry

    lax.fori_loop(0, count // group, row_terms, 0)
    rows_in[...] = row_sums[...].astype(bf)
    mine_at = piece(b, a)
    for h in range(cuts):
        at = pl.ds(h * sub, sub)
        pair_copies[0, h].wait_recv()
        mine = part[sub_span(mine_at, h)].astype(jnp.float32)
        yz_sum[at] = mine + pair_in[m - 1, h].astype(jnp.float32)
    for d in near:
        for h in range(cuts):

            @pl.when(valid(-d))
            def _():
                at = pl.ds(h * sub, sub)
                line_copies[d, h].wait_recv()
                yz_sum[at] = yz_sum[at] + line_in[d + m - 1, h].astype(jnp.float32)

    yz_plane[pl.ds(reach * chans, rows * chans), :] = yz_sum[...].astype(bf).reshape(rows * chans, cols)

    place = g * n + mine_at
    last = 2 * n - 1
    edge = reach * chans
    before = jnp.maximum(place - 1, 0)
    after = jnp.minimum(place + 1, last)
    up = pltpu.make_async_remote_copy(
        src_ref=yz_plane.at[pl.ds(edge, edge)],
        dst_ref=yz_plane.at[pl.ds(edge + rows * chans, edge)],
        send_sem=halo_s.at[0],
        recv_sem=halo_r.at[0],
        device_id={"gx": owner(before % n), "gy": before // n},
        device_id_type=MESH,
    )
    down = pltpu.make_async_remote_copy(
        src_ref=yz_plane.at[pl.ds(rows * chans, edge)],
        dst_ref=yz_plane.at[pl.ds(0, edge)],
        send_sem=halo_s.at[1],
        recv_sem=halo_r.at[1],
        device_id={"gx": owner(after % n), "gy": after // n},
        device_id_type=MESH,
    )
    pl.when(place > 0)(up.start)
    pl.when(place < last)(down.start)
    for dx, copy in row_copies:
        pl.when((me + dx >= 0) & (me + dx < n))(copy.start)

    @pl.when(place == 0)
    def _():
        yz_plane[pl.ds(0, edge), :] = jnp.zeros((edge, cols), jnp.bfloat16)

    @pl.when(place == last)
    def _():
        yz_plane[pl.ds(edge + rows * chans, edge), :] = jnp.zeros((edge, cols), jnp.bfloat16)

    def inner_row(i, keep):
        window = yz_plane[pl.ds(pl.multiple_of(i * chans, chans), 3 * chans), :]
        inner = silu(conv_row(window, weights[2, 0])) * keep
        yz_inner[pl.ds(pl.multiple_of(i * chans, chans), chans), :] = inner.astype(jnp.bfloat16)

    for i in range(reach, rows):
        inner_row(i, 1.0)
    pl.when(place < last)(up.wait_recv)
    pl.when(place > 0)(down.wait_recv)
    for i in list(range(reach)) + list(range(rows, rows + 2)):
        keep = 1.0
        if i == 0:
            keep = (place > 0).astype(jnp.float32)
        if i == rows + 1:
            keep = (place < last).astype(jnp.float32)
        inner_row(i, keep)
    def give(j, h, sems, at, target):
        return pltpu.make_async_remote_copy(
            src_ref=yz_out.at[sub_span(j, h)],
            dst_ref=yz_out.at[sub_span(j, h)],
            send_sem=sems[0].at[at, h],
            recv_sem=sems[1].at[at, h],
            device_id={"gx": target},
            device_id_type=MESH,
        )

    spread = (spread_s, spread_r)
    cross = (cross_s, cross_r)
    sends = []
    for h in range(cuts):
        for r in range(h * sub, (h + 1) * sub):
            done = conv_row(yz_inner[pl.ds(r * chans, 3 * chans), :], weights[2, 1])
            yz_out[mine_at * rows + r] = done.astype(bf)
        for d in near:
            copy = give(mine_at, h, spread, d + m - 1, spot(d) * 2 + b)
            pl.when(valid(d))(copy.start)
            sends.append((d, copy))
        copy = give(mine_at, h, cross, m - 1, partner)
        copy.start()
        sends.append((0, copy))

    for dx, copy in row_copies:
        pl.when((me - dx >= 0) & (me - dx < n))(copy.wait_recv)
    planes = rows_in.shape[0]
    for s in range(2 * reach + 1):
        at = me + s - reach
        inside = (at >= 0) & (at < n)
        here = pl.ds(s * chans, chans)

        @pl.when(inside)
        def _():
            first = rows_in[...] if s == reach else row_slots[s, 0]
            total = first.astype(jnp.float32) + row_slots[s, 1].astype(jnp.float32)
            row_plane[:, here, :] = total.astype(jnp.bfloat16)

        @pl.when(jnp.logical_not(inside))
        def _():
            row_plane[:, here, :] = jnp.zeros((planes, chans, cols), jnp.bfloat16)

    for p in range(planes):
        for s in range(3):
            at = me + s - 1
            keep = ((at >= 0) & (at < n)).astype(jnp.float32)
            inner = silu(conv_row(row_plane[p, s * chans : (s + 3) * chans, :], weights[p, 0]))
            row_inner[p, s * chans : (s + 1) * chans, :] = (inner * keep).astype(jnp.bfloat16)
    xy_out[...] = conv_row(row_inner[0], weights[0, 1]).astype(bf).astype(jnp.float32)
    xz_out[...] = conv_row(row_inner[1], weights[1, 1]).astype(bf).astype(jnp.float32)

    step_rows = 4 if sub % 4 == 0 else (2 if sub % 2 == 0 else 1)

    def finish(j, h):
        def some_rows(step, carry):
            at = [j * rows + h * sub + step * step_rows + k for k in range(step_rows)]
            mixed = []
            for y in at:
                product = column(xy_out[...], g * count + y) * xz_out[...]
                product = product * yz_out[y].astype(jnp.float32)
                mixed.append((product_scale * product).astype(bf))
            mixed = jnp.concatenate(mixed, axis=1)
            hidden = silu(jnp.dot(wide[...], mixed, preferred_element_type=jnp.float32)).astype(bf)
            branch = jnp.dot(shrink[...], hidden, preferred_element_type=jnp.float32)
            for k, y in enumerate(at):
                updated[y] = (feature_row(y) + branch[:, k * cols : (k + 1) * cols]).astype(bf)
            return carry

        lax.fori_loop(0, sub // step_rows, some_rows, 0)

    for h in range(cuts):
        finish(mine_at, h)
    for h in range(cuts):
        for d in near:

            @pl.when(valid(d))
            def _():
                j = piece(b, spot(d))
                give(j, h, spread, m - 1 - d, partner).wait_recv()
                give(j, h, cross, m - 1 + d, partner).start()
                finish(j, h)

    for h in range(cuts):
        for d in [0] + near:

            @pl.when(valid(d))
            def _():
                j = piece(1 - b, spot(d))
                give(j, h, cross, m - 1 + d, partner).wait_recv()
                finish(j, h)

    for d in near:
        for h in range(cuts):
            pl.when(valid(d))(give(piece(b, spot(d)), h, cross, m - 1 + d, partner).wait_send)
    for d, copy in sends:
        pl.when(valid(d))(copy.wait_send)
    for (d, h), copy in list(pair_copies.items()) + list(line_copies.items()):
        pl.when(valid(d))(copy.wait_send)
    for dx, copy in row_copies:
        pl.when((me + dx >= 0) & (me + dx < n))(copy.wait_send)
    pl.when(place > 0)(up.wait_send)
    pl.when(place < last)(down.wait_send)


def fused(voxels, occupancy, row_weights, column_weights, depth_weights, plane_kernels, expand_weight, shrink_weight):
    n = lax.axis_size("gx")
    m = n // 2
    count, cols, chans = voxels.shape[1:]
    rows = count // n
    sets, layers = plane_kernels.shape[:2]
    planes = 2
    span = 2 * reach + 1
    bf = jnp.bfloat16
    f32 = jnp.float32
    dma = pltpu.SemaphoreType.DMA
    block = dma((2 * m - 1, cuts))
    updated = pl.pallas_call(
        functools.partial(block_kernel, n),
        out_shape=pltpu.VMEM((count, chans, cols), bf),
        in_specs=[pl.BlockSpec(memory_space=pltpu.VMEM)] * 8,
        out_specs=pl.BlockSpec(memory_space=pltpu.VMEM),
        scratch_shapes=[
            pltpu.VMEM((count, chans, cols), bf),
            pltpu.VMEM((planes, chans, cols), bf),
            pltpu.VMEM((sets, layers, 3 * chans, 3 * chans), bf),
            pltpu.VMEM(expand_weight.shape[::-1], bf),
            pltpu.VMEM((count, chans, cols), bf),
            pltpu.VMEM((chans, 2 * count), f32),
            pltpu.VMEM((chans, cols), f32),
            pltpu.VMEM((planes, chans, cols), f32),
            pltpu.VMEM((chans, count), f32),
            pltpu.VMEM((2 * m - 1, cuts, rows // cuts, chans, cols), bf),
            pltpu.VMEM((2 * m - 1, cuts, rows // cuts, chans, cols), bf),
            pltpu.VMEM((2 * m - 1, cuts, rows // cuts, chans, cols), bf),
            pltpu.VMEM((rows, chans, cols), f32),
            pltpu.VMEM(((rows + 4) * chans, cols), bf),
            pltpu.VMEM(((rows + 2) * chans, cols), bf),
            pltpu.VMEM((span, 2, planes, chans, cols), bf),
            pltpu.VMEM((planes, span * chans, cols), bf),
            pltpu.VMEM((planes, 3 * chans, cols), bf),
            block, block, block, block, dma((2,)), dma((2,)),
            dma((span, 2)), dma((span, 2)), block, block, block, block,
        ],
        compiler_params=pltpu.CompilerParams(collective_id=0, has_side_effects=True),
    )(
        voxels[0].transpose(0, 2, 1),
        occupancy[0],
        row_weights,
        column_weights,
        depth_weights.T,
        plane_kernels,
        expand_weight,
        shrink_weight.T,
    )
    return updated.transpose(0, 2, 1)[None]


def fits(voxels):
    n = lax.axis_size("gx")
    sides = lax.axis_size("gy")
    xs, ys, zs, _ = voxels.shape
    return xs == 1 and sides == 2 and n % 2 == 0 and n >= 4 and ys % n == 0 and ys // n >= reach and ys // n % cuts == 0 and 2 * ys == zs


def plain_planes(features, row_weights, column_weights, depth_weights, plane_kernels):
    xy_plane = jnp.einsum(
        "xyzc,zc->xyc", features, depth_weights, preferred_element_type=jnp.float32
    ).astype(jnp.bfloat16)
    xz_part = jnp.einsum(
        "xyzc,yc->xzc", features, column_weights, preferred_element_type=jnp.float32
    )
    yz_part = jnp.einsum("xyzc,xc->yzc", features, row_weights, preferred_element_type=jnp.float32)
    xy_out = plane_block(xy_plane, plane_kernels[0], rim_xy)
    xz_plane = lax.psum(xz_part, "gy").astype(jnp.bfloat16)
    xz_out = plane_block(xz_plane, plane_kernels[1], rim_xz)
    yz_plane = lax.psum(yz_part, "gx").astype(jnp.bfloat16)
    yz_out = plane_block(yz_plane, plane_kernels[2], rim_yz)
    return xy_out, xz_out, yz_out


def shards(
    voxels,
    occupancy,
    row_weights,
    column_weights,
    depth_weights,
    plane_kernels,
    expand_weight,
    shrink_weight,
):
    if fits(voxels):
        return fused(
            voxels,
            occupancy,
            row_weights,
            column_weights,
            depth_weights,
            plane_kernels,
            expand_weight,
            shrink_weight,
        )
    features = voxels * occupancy.astype(jnp.bfloat16)[..., None]
    xy_out, xz_out, yz_out = plain_planes(features, row_weights, column_weights, depth_weights, plane_kernels)
    product = xy_out.astype(jnp.float32)[:, :, None, :] * xz_out.astype(jnp.float32)[:, None, :, :]
    product = product * yz_out.astype(jnp.float32)[None, :, :, :]
    mixed = (product_scale * product).astype(jnp.bfloat16)
    hidden = jax.nn.silu(
        jnp.einsum("xyzc,ch->xyzh", mixed, expand_weight, preferred_element_type=jnp.float32)
    ).astype(jnp.bfloat16)
    branch = jnp.einsum("xyzh,hc->xyzc", hidden, shrink_weight, preferred_element_type=jnp.float32)
    return (features.astype(jnp.float32) + branch).astype(jnp.bfloat16)


def solution(mesh):
    in_specs = (
        P(("groups", "gx"), "gy", None, None),
        P(("groups", "gx"), "gy", None),
        P("gx", None),
        P("gy", None),
        P(),
        P(),
        P(),
        P(),
    )
    out_specs = P(("groups", "gx"), "gy", None, None)
    return jax.shard_map(shards, mesh=mesh, in_specs=in_specs, out_specs=out_specs, check_vma=False)
```

```python
import functools

import jax
import jax.numpy as jnp
from jax import lax
from jax.experimental import pallas as pl
from jax.experimental.pallas import tpu as pltpu
from jax.sharding import PartitionSpec as P

MESH = pl.DeviceIdType.MESH
reach = 2
cuts = 2

product_scale = 8.0


def with_halo(cells, sides, width):
    for axis, dim in sides:
        count = lax.axis_size(axis)
        ends = count - 1
        head = lax.slice_in_dim(cells, 0, width, axis=dim)
        tail = lax.slice_in_dim(cells, cells.shape[dim] - width, cells.shape[dim], axis=dim)
        cells = jnp.concatenate(
            [
                lax.ppermute(tail, axis, [(i, (i + 1) % count) for i in range(ends)]),
                cells,
                lax.ppermute(head, axis, [((i + 1) % count, i) for i in range(ends)]),
            ],
            axis=dim,
        )
    return cells


def conv_valid(padded, kernel):
    rows = padded.shape[0] - 2
    cols = padded.shape[1] - 2
    total = jnp.zeros((rows, cols, kernel.shape[-1]), jnp.float32)
    for row_off in range(3):
        for col_off in range(3):
            window = padded[row_off : row_off + rows, col_off : col_off + cols]
            total = total + jnp.einsum(
                "ijc,co->ijo", window, kernel[row_off, col_off], preferred_element_type=jnp.float32
            )
    return total


def plane_block(plane, kernels, extend):
    inner = jax.nn.silu(conv_valid(extend(plane), kernels[0])).astype(jnp.bfloat16)
    return conv_valid(extend(inner), kernels[1]).astype(jnp.bfloat16)


def rim_xy(plane):
    return with_halo(plane, (("gx", 0), ("gy", 1)), 1)


def rim_xz(plane):
    padded = with_halo(plane, (("gx", 0),), 1)
    return jnp.pad(padded, ((0, 0), (1, 1), (0, 0)))


def rim_yz(plane):
    padded = with_halo(plane, (("gy", 0),), 1)
    return jnp.pad(padded, ((0, 0), (1, 1), (0, 0)))


def conv_row(window, weight):
    taps = jnp.dot(weight, window, preferred_element_type=jnp.float32)
    chans = taps.shape[0] // 3
    cols = taps.shape[1]
    lane = lax.broadcasted_iota(jnp.int32, (chans, cols), 1)
    left = pltpu.roll(taps[:chans], 1, 1)
    right = pltpu.roll(taps[2 * chans :], cols - 1, 1)
    left = jnp.where(lane == 0, 0.0, left)
    right = jnp.where(lane == cols - 1, 0.0, right)
    return taps[chans : 2 * chans] + left + right


def silu(v):
    return v / (1.0 + jnp.exp(-v))


def identity(size):
    row = lax.broadcasted_iota(jnp.int32, (size, size), 0)
    col = lax.broadcasted_iota(jnp.int32, (size, size), 1)
    return jnp.where(row == col, 1.0, 0.0)


def flipped(x):
    eye = identity(x.shape[1]).astype(x.dtype)
    return lax.dot_general(eye, x, (((1,), (1,)), ((), ())), preferred_element_type=jnp.float32)


def column(x, at):
    lane = lax.broadcasted_iota(jnp.int32, x.shape, 1)
    return jnp.sum(jnp.where(lane == at, x, 0.0), axis=1, keepdims=True)


def block_kernel(
    n, voxels, occupancy, row_weights, column_weights, depth_weights, kernels_in, expand, shrink, updated,
    plane_kernels, fetch_s,
    part, rows_in, weights, wide, yz_out, xy_out, xz_out, row_sums, turned,
    pair_in, pair_sum, line_in, yz_sum, yz_plane, yz_inner, row_slots, row_plane, row_inner,
    pair_s, pair_r, line_s, line_r, halo_s, halo_r, row_s, row_r, spread_s, spread_r, cross_s, cross_r,
):
    me = lax.axis_index("gx")
    g = lax.axis_index("gy")
    m = n // 2
    a = me // 2
    b = me % 2
    count, chans, cols = part.shape
    rows = count // n
    bf = jnp.bfloat16

    def feature_row(y):
        return voxels[y].astype(jnp.float32) * occupancy[pl.ds(y, 1), :].astype(jnp.float32)

    def piece(bb, aa):
        return bb * m + aa + bb * (m - 1 - 2 * aa)

    def owner(j):
        bb = j // m
        aa = j % m
        return (aa + bb * (m - 1 - 2 * aa)) * 2 + bb

    def span(j):
        return pl.ds(j * rows, rows)

    fetch = pltpu.make_async_copy(kernels_in, plane_kernels, fetch_s)
    fetch.start()
    barrier = pltpu.get_barrier_semaphore()
    for step in range(1, 2 * n):
        spot = (me * 2 + g + step) % (2 * n)
        pl.semaphore_signal(barrier, inc=1, device_id={"gx": spot // 2, "gy": spot % 2}, device_id_type=MESH)

    rw = jnp.broadcast_to(row_weights[...].astype(jnp.float32), (chans, chans))
    rw = jnp.sum(rw * identity(chans), axis=1, keepdims=True)
    group = 4 if rows % 4 == 0 else 2

    def yz_terms(step, carry):
        for k in range(group):
            y = step * group + k
            part[y] = (feature_row(y) * rw).astype(bf)
        return carry

    lax.fori_loop(0, count // group, yz_terms, 0)
    pl.semaphore_wait(barrier, 2 * n - 1)

    row_copies = []
    for dx in range(-reach, reach + 1):
        for dg in range(2):
            if dx == 0 and dg == 0:
                continue
            slot = reach - dx
            copy = pltpu.make_async_remote_copy(
                src_ref=rows_in,
                dst_ref=row_slots.at[slot, dg],
                send_sem=row_s.at[slot, dg],
                recv_sem=row_r.at[slot, dg],
                device_id={"gx": jnp.clip(me + dx, 0, n - 1), "gy": (g + dg) % 2},
                device_id_type=MESH,
            )
            row_copies.append((dx, copy))

    sub = rows // cuts
    far = sorted([d for d in range(1 - m, m) if d != 0], key=lambda d: -abs(d))
    near = far[::-1]
    partner = a * 2 + 1 - b

    def valid(d):
        return (a + d >= 0) & (a + d < m)

    def spot(d):
        return jnp.clip(a + d, 0, m - 1)

    def sub_span(j, h):
        return pl.ds(j * rows + h * sub, sub)

    pair_copies = {}
    line_copies = {}
    for d in far + [0]:
        for h in range(cuts):
            pair_copies[d, h] = pltpu.make_async_remote_copy(
                src_ref=part.at[sub_span(piece(1 - b, spot(d)), h)],
                dst_ref=pair_in.at[d + m - 1, h],
                send_sem=pair_s.at[d + m - 1, h],
                recv_sem=pair_r.at[d + m - 1, h],
                device_id={"gx": partner},
                device_id_type=MESH,
            )
            if d != 0:
                line_copies[d, h] = pltpu.make_async_remote_copy(
                    src_ref=pair_sum.at[d + m - 1, h],
                    dst_ref=line_in.at[d + m - 1, h],
                    send_sem=line_s.at[d + m - 1, h],
                    recv_sem=line_r.at[d + m - 1, h],
                    device_id={"gx": spot(d) * 2 + b},
                    device_id_type=MESH,
                )
    for (d, h), copy in pair_copies.items():
        pl.when(valid(d))(copy.start)
    for d in far:
        for h in range(cuts):

            @pl.when(valid(d))
            def _():
                pair_copies[d, h].wait_recv()
                mine = part[sub_span(piece(b, spot(d)), h)].astype(jnp.float32)
                pair_sum[d + m - 1, h] = (mine + pair_in[d + m - 1, h].astype(jnp.float32)).astype(bf)
                line_copies[d, h].start()

    fetch.wait()
    turned[...] = flipped(column_weights[...])
    wide[...] = flipped(expand[...]).astype(bf)
    for p in range(plane_kernels.shape[0]):
        for layer in range(2):
            for off in range(3):
                taps = plane_kernels[p, layer, :, off].reshape(3 * chans, chans)
                weights[p, layer, off * chans : (off + 1) * chans, :] = flipped(taps).astype(bf)

    row_sums[...] = jnp.zeros(row_sums.shape, jnp.float32)
    depth = depth_weights[...].astype(jnp.float32)
    lane = lax.broadcasted_iota(jnp.int32, (chans, cols), 1)

    def row_terms(step, carry):
        xy, xz = row_sums[0], row_sums[1]
        for k in range(group):
            y = step * group + k
            f = feature_row(y)
            xy = jnp.where(lane == g * count + y, jnp.sum(f * depth, axis=1, keepdims=True), xy)
            xz = xz + f * column(turned[...], y)
        row_sums[0] = xy
        row_sums[1] = xz
        return carry

    lax.fori_loop(0, count // group, row_terms, 0)
    rows_in[...] = row_sums[...].astype(bf)
    mine_at = piece(b, a)
    for h in range(cuts):
        at = pl.ds(h * sub, sub)
        pair_copies[0, h].wait_recv()
        mine = part[sub_span(mine_at, h)].astype(jnp.float32)
        yz_sum[at] = mine + pair_in[m - 1, h].astype(jnp.float32)
    for d in near:
        for h in range(cuts):

            @pl.when(valid(-d))
            def _():
                at = pl.ds(h * sub, sub)
                line_copies[d, h].wait_recv()
                yz_sum[at] = yz_sum[at] + line_in[d + m - 1, h].astype(jnp.float32)

    yz_plane[pl.ds(reach * chans, rows * chans), :] = yz_sum[...].astype(bf).reshape(rows * chans, cols)

    place = g * n + mine_at
    last = 2 * n - 1
    edge = reach * chans
    before = jnp.maximum(place - 1, 0)
    after = jnp.minimum(place + 1, last)
    up = pltpu.make_async_remote_copy(
        src_ref=yz_plane.at[pl.ds(edge, edge)],
        dst_ref=yz_plane.at[pl.ds(edge + rows * chans, edge)],
        send_sem=halo_s.at[0],
        recv_sem=halo_r.at[0],
        device_id={"gx": owner(before % n), "gy": before // n},
        device_id_type=MESH,
    )
    down = pltpu.make_async_remote_copy(
        src_ref=yz_plane.at[pl.ds(rows * chans, edge)],
        dst_ref=yz_plane.at[pl.ds(0, edge)],
        send_sem=halo_s.at[1],
        recv_sem=halo_r.at[1],
        device_id={"gx": owner(after % n), "gy": after // n},
        device_id_type=MESH,
    )
    pl.when(place > 0)(up.start)
    pl.when(place < last)(down.start)
    for dx, copy in row_copies:
        pl.when((me + dx >= 0) & (me + dx < n))(copy.start)

    @pl.when(place == 0)
    def _():
        yz_plane[pl.ds(0, edge), :] = jnp.zeros((edge, cols), jnp.bfloat16)

    @pl.when(place == last)
    def _():
        yz_plane[pl.ds(edge + rows * chans, edge), :] = jnp.zeros((edge, cols), jnp.bfloat16)

    def inner_row(i, keep):
        window = yz_plane[pl.ds(pl.multiple_of(i * chans, chans), 3 * chans), :]
        inner = silu(conv_row(window, weights[2, 0])) * keep
        yz_inner[pl.ds(pl.multiple_of(i * chans, chans), chans), :] = inner.astype(jnp.bfloat16)

    for i in range(reach, rows):
        inner_row(i, 1.0)
    pl.when(place < last)(up.wait_recv)
    pl.when(place > 0)(down.wait_recv)
    for i in list(range(reach)) + list(range(rows, rows + 2)):
        keep = 1.0
        if i == 0:
            keep = (place > 0).astype(jnp.float32)
        if i == rows + 1:
            keep = (place < last).astype(jnp.float32)
        inner_row(i, keep)
    def give(j, h, sems, at, target):
        return pltpu.make_async_remote_copy(
            src_ref=yz_out.at[sub_span(j, h)],
            dst_ref=yz_out.at[sub_span(j, h)],
            send_sem=sems[0].at[at, h],
            recv_sem=sems[1].at[at, h],
            device_id={"gx": target},
            device_id_type=MESH,
        )

    spread = (spread_s, spread_r)
    cross = (cross_s, cross_r)
    sends = []
    for h in range(cuts):
        for r in range(h * sub, (h + 1) * sub):
            done = conv_row(yz_inner[pl.ds(r * chans, 3 * chans), :], weights[2, 1])
            yz_out[mine_at * rows + r] = done.astype(bf)
        for d in near:
            copy = give(mine_at, h, spread, d + m - 1, spot(d) * 2 + b)
            pl.when(valid(d))(copy.start)
            sends.append((d, copy))
        copy = give(mine_at, h, cross, m - 1, partner)
        copy.start()
        sends.append((0, copy))

    for dx, copy in row_copies:
        pl.when((me - dx >= 0) & (me - dx < n))(copy.wait_recv)
    planes = rows_in.shape[0]
    for s in range(2 * reach + 1):
        at = me + s - reach
        inside = (at >= 0) & (at < n)
        here = pl.ds(s * chans, chans)

        @pl.when(inside)
        def _():
            first = rows_in[...] if s == reach else row_slots[s, 0]
            total = first.astype(jnp.float32) + row_slots[s, 1].astype(jnp.float32)
            row_plane[:, here, :] = total.astype(jnp.bfloat16)

        @pl.when(jnp.logical_not(inside))
        def _():
            row_plane[:, here, :] = jnp.zeros((planes, chans, cols), jnp.bfloat16)

    for p in range(planes):
        for s in range(3):
            at = me + s - 1
            keep = ((at >= 0) & (at < n)).astype(jnp.float32)
            inner = silu(conv_row(row_plane[p, s * chans : (s + 3) * chans, :], weights[p, 0]))
            row_inner[p, s * chans : (s + 1) * chans, :] = (inner * keep).astype(jnp.bfloat16)
    xy_out[...] = conv_row(row_inner[0], weights[0, 1]).astype(bf).astype(jnp.float32)
    xz_out[...] = conv_row(row_inner[1], weights[1, 1]).astype(bf).astype(jnp.float32)

    step_rows = 4 if sub % 4 == 0 else (2 if sub % 2 == 0 else 1)

    def finish(j, h):
        def some_rows(step, carry):
            at = [j * rows + h * sub + step * step_rows + k for k in range(step_rows)]
            mixed = []
            for y in at:
                product = column(xy_out[...], g * count + y) * xz_out[...]
                product = product * yz_out[y].astype(jnp.float32)
                mixed.append((product_scale * product).astype(bf))
            mixed = jnp.concatenate(mixed, axis=1)
            hidden = silu(jnp.dot(wide[...], mixed, preferred_element_type=jnp.float32)).astype(bf)
            branch = jnp.dot(shrink[...], hidden, preferred_element_type=jnp.float32)
            for k, y in enumerate(at):
                updated[y] = (feature_row(y) + branch[:, k * cols : (k + 1) * cols]).astype(bf)
            return carry

        lax.fori_loop(0, sub // step_rows, some_rows, 0)

    for h in range(cuts):
        finish(mine_at, h)
    for h in range(cuts):
        for d in near:

            @pl.when(valid(d))
            def _():
                j = piece(b, spot(d))
                give(j, h, spread, m - 1 - d, partner).wait_recv()
                give(j, h, cross, m - 1 + d, partner).start()
                finish(j, h)

    for h in range(cuts):
        for d in [0] + near:

            @pl.when(valid(d))
            def _():
                j = piece(1 - b, spot(d))
                give(j, h, cross, m - 1 + d, partner).wait_recv()
                finish(j, h)

    for d in near:
        for h in range(cuts):
            pl.when(valid(d))(give(piece(b, spot(d)), h, cross, m - 1 + d, partner).wait_send)
    for d, copy in sends:
        pl.when(valid(d))(copy.wait_send)
    for (d, h), copy in list(pair_copies.items()) + list(line_copies.items()):
        pl.when(valid(d))(copy.wait_send)
    for dx, copy in row_copies:
        pl.when((me + dx >= 0) & (me + dx < n))(copy.wait_send)
    pl.when(place > 0)(up.wait_send)
    pl.when(place < last)(down.wait_send)


def fused(voxels, occupancy, row_weights, column_weights, depth_weights, plane_kernels, expand_weight, shrink_weight):
    n = lax.axis_size("gx")
    m = n // 2
    count, cols, chans = voxels.shape[1:]
    rows = count // n
    sets, layers = plane_kernels.shape[:2]
    planes = 2
    span = 2 * reach + 1
    bf = jnp.bfloat16
    f32 = jnp.float32
    dma = pltpu.SemaphoreType.DMA
    block = dma((2 * m - 1, cuts))
    updated = pl.pallas_call(
        functools.partial(block_kernel, n),
        out_shape=pltpu.VMEM((count, chans, cols), bf),
        in_specs=[pl.BlockSpec(memory_space=pl.ANY if k == 5 else pltpu.VMEM) for k in range(8)],
        out_specs=pl.BlockSpec(memory_space=pltpu.VMEM),
        scratch_shapes=[
            pltpu.VMEM(plane_kernels.shape, bf),
            dma,
            pltpu.VMEM((count, chans, cols), bf),
            pltpu.VMEM((planes, chans, cols), bf),
            pltpu.VMEM((sets, layers, 3 * chans, 3 * chans), bf),
            pltpu.VMEM(expand_weight.shape[::-1], bf),
            pltpu.VMEM((count, chans, cols), bf),
            pltpu.VMEM((chans, 2 * count), f32),
            pltpu.VMEM((chans, cols), f32),
            pltpu.VMEM((planes, chans, cols), f32),
            pltpu.VMEM((chans, count), f32),
            pltpu.VMEM((2 * m - 1, cuts, rows // cuts, chans, cols), bf),
            pltpu.VMEM((2 * m - 1, cuts, rows // cuts, chans, cols), bf),
            pltpu.VMEM((2 * m - 1, cuts, rows // cuts, chans, cols), bf),
            pltpu.VMEM((rows, chans, cols), f32),
            pltpu.VMEM(((rows + 4) * chans, cols), bf),
            pltpu.VMEM(((rows + 2) * chans, cols), bf),
            pltpu.VMEM((span, 2, planes, chans, cols), bf),
            pltpu.VMEM((planes, span * chans, cols), bf),
            pltpu.VMEM((planes, 3 * chans, cols), bf),
            block, block, block, block, dma((2,)), dma((2,)),
            dma((span, 2)), dma((span, 2)), block, block, block, block,
        ],
        compiler_params=pltpu.CompilerParams(collective_id=0, has_side_effects=True),
    )(
        voxels[0].transpose(0, 2, 1),
        occupancy[0],
        row_weights,
        column_weights,
        depth_weights.T,
        plane_kernels,
        expand_weight,
        shrink_weight.T,
    )
    return updated.transpose(0, 2, 1)[None]


def fits(voxels):
    n = lax.axis_size("gx")
    sides = lax.axis_size("gy")
    xs, ys, zs, _ = voxels.shape
    return xs == 1 and sides == 2 and n % 2 == 0 and n >= 4 and ys % n == 0 and ys // n >= reach and ys // n % cuts == 0 and 2 * ys == zs


def plain_planes(features, row_weights, column_weights, depth_weights, plane_kernels):
    xy_plane = jnp.einsum(
        "xyzc,zc->xyc", features, depth_weights, preferred_element_type=jnp.float32
    ).astype(jnp.bfloat16)
    xz_part = jnp.einsum(
        "xyzc,yc->xzc", features, column_weights, preferred_element_type=jnp.float32
    )
    yz_part = jnp.einsum("xyzc,xc->yzc", features, row_weights, preferred_element_type=jnp.float32)
    xy_out = plane_block(xy_plane, plane_kernels[0], rim_xy)
    xz_plane = lax.psum(xz_part, "gy").astype(jnp.bfloat16)
    xz_out = plane_block(xz_plane, plane_kernels[1], rim_xz)
    yz_plane = lax.psum(yz_part, "gx").astype(jnp.bfloat16)
    yz_out = plane_block(yz_plane, plane_kernels[2], rim_yz)
    return xy_out, xz_out, yz_out


def shards(
    voxels,
    occupancy,
    row_weights,
    column_weights,
    depth_weights,
    plane_kernels,
    expand_weight,
    shrink_weight,
):
    if fits(voxels):
        return fused(
            voxels,
            occupancy,
            row_weights,
            column_weights,
            depth_weights,
            plane_kernels,
            expand_weight,
            shrink_weight,
        )
    features = voxels * occupancy.astype(jnp.bfloat16)[..., None]
    xy_out, xz_out, yz_out = plain_planes(features, row_weights, column_weights, depth_weights, plane_kernels)
    product = xy_out.astype(jnp.float32)[:, :, None, :] * xz_out.astype(jnp.float32)[:, None, :, :]
    product = product * yz_out.astype(jnp.float32)[None, :, :, :]
    mixed = (product_scale * product).astype(jnp.bfloat16)
    hidden = jax.nn.silu(
        jnp.einsum("xyzc,ch->xyzh", mixed, expand_weight, preferred_element_type=jnp.float32)
    ).astype(jnp.bfloat16)
    branch = jnp.einsum("xyzh,hc->xyzc", hidden, shrink_weight, preferred_element_type=jnp.float32)
    return (features.astype(jnp.float32) + branch).astype(jnp.bfloat16)


def solution(mesh):
    in_specs = (
        P(("groups", "gx"), "gy", None, None),
        P(("groups", "gx"), "gy", None),
        P("gx", None),
        P("gy", None),
        P(),
        P(),
        P(),
        P(),
    )
    out_specs = P(("groups", "gx"), "gy", None, None)
    return jax.shard_map(shards, mesh=mesh, in_specs=in_specs, out_specs=out_specs, check_vma=False)
```
